512 devices in a mesh: pair: 2 (over x_lo), row: 16 (over y, x_hi), col: 16 (over z, core).
Axes of the slice: x: 4 (x_hi: 2, x_lo: 2; x = x_hi * 2 + x_lo), y: 8, z: 8, core: 2. Of those that a mesh axis runs over, the one named last changes fastest.
Arguments:
- features: bfloat16 [2, 64, 256, 2048], P('pair', None, 'row', 'col'), may hold values from -6 to 6
- offsets: int32 [2, 2, 256, 2048], P('pair', None, 'row', 'col'), may hold values from -8 to 7
- fractions: int32 [2, 2, 256, 2048], P('pair', None, 'row', 'col'), may hold values from 0 to 255
- tissue: int32 [2, 32, 256], P('pair', 'row', 'col'), may hold values 0 or 1
- w_first: bfloat16 [9, 64, 128], replicated, may hold values from -0.1875 to 0.1875
- w_second: bfloat16 [9, 64, 64], replicated, may hold values from -0.25 to 0.25
- head_weight: bfloat16 [2, 64], replicated, may hold values from -0.75 to 0.75
Outputs:
- warped_features: bfloat16 [2, 64, 256, 2048], P('pair', None, 'row', 'col')
- motion_field: float32 [2, 2, 256, 2048], P('pair', None, 'row', 'col')
The draws below stay inside these ranges and needn't reach their ends.
All inputs are finite; a program needn't handle non-finite values. No bound on the sum of `tissue` on one device may be relied on, other than what follows from the above.
Results may differ from the reference program's by a relative error of at most 0.0056.
Values may be sent and summed in bfloat16 or wider, within the bound.
No kernel may reach another device: no remote copies, remote signals or barrier semaphores. Data moves between devices by JAX's collectives and lax.ppermute only.
A program may use at most 64 MiB of HBM per device.

```python
import jax
import jax.numpy as jnp
from jax import lax

C = 64
MAXS = 8
BLK = 8
NR = 256
NC = 2048


def draw_offsets(key, part):
    values = jax.random.randint(key, (2, 2, NR, NC), -MAXS, MAXS, dtype=jnp.int32)
    values = values.at[0, 0, 0, 0].set(-MAXS)
    values = values.at[1, 1, NR - 1, NC - 1].set(MAXS - 1)
    return values


def plant(result, own_key, smallest, high):
    longest = result.shape.index(max(result.shape))
    spots = []
    for shift in (0, 1):
        where = [jax.random.randint(jax.random.fold_in(own_key, axis), (), 0, length) for axis, length in enumerate(result.shape)]
        where[longest] = (where[longest] + shift) % result.shape[longest]
        spots.append(tuple(where))
    return result.at[spots[0]].set(smallest).at[spots[1]].set(high)


def block_levels(rng, dims, shards, smallest, largest):
    def one(dim, shards_of):
        steps = jax.random.uniform(jax.random.fold_in(jax.random.fold_in(rng, 6), dim), (shards_of,), jnp.float32, smallest / len(shards), largest / len(shards))
        return jnp.repeat(jnp.exp(steps), dims[dim] // shards_of).reshape((-1,) + (1,) * (len(dims) - dim - 1))

    gain = one(*shards[0])
    for cut in shards[1:]:
        gain = gain * one(*cut)
    return gain


def centred(own_key, shape, deviation, most, cuts=(), held_as=jnp.bfloat16):
    gain = block_levels(own_key, shape, cuts, -0.22, 0.18) if cuts else 1.0
    values = jax.random.normal(own_key, shape, jnp.float32) * deviation * gain
    return jnp.minimum(jnp.maximum(values, -most), most).astype(held_as)


def setup_inputs(seed: int = 0) -> dict:
    key_list = jax.random.split(jax.random.key(seed), 8)
    return {
        "features": centred(key_list[0], (2, C, NR, NC), 1.0, 6.0, ((0, 2), (2, 16), (3, 16))),
        "offsets": draw_offsets(jax.random.fold_in(key_list[7], 71), 0),
        "fractions": plant(jax.random.randint(key_list[2], (2, 2, NR, NC), 0, 256), jax.random.fold_in(key_list[2], 1), 0, 255).astype(jnp.int32),
        "tissue": plant((jax.random.randint(key_list[3], (2, NR // BLK, NC // BLK), 0, 4) < 3).astype(jnp.int32), jax.random.fold_in(key_list[3], 1), 0, 1),
        "w_first": centred(key_list[4], (9, C, 2 * C), (18 * C) ** -0.5, 0.1875),
        "w_second": centred(key_list[5], (9, C, C), (9 * C) ** -0.5, 0.25),
        "head_weight": centred(key_list[6], (2, C), C ** -0.5, 0.75),
    }


frac_scale = 256.0


def convolve(padded, weights, height, columns):
    summed = None
    for tap_index in range(9):
        row_shift = tap_index // 3
        col_shift = tap_index % 3
        window = padded[:, row_shift:row_shift + height, col_shift:col_shift + columns]
        window = window.reshape(padded.shape[0], height * columns)
        product = jnp.dot(weights[tap_index], window, preferred_element_type=jnp.float32)
        summed = product if summed is None else summed + product
    return summed.reshape(weights.shape[1], height, columns)


def sample(source, motion, margin, height, columns):
    stride = columns + 2 * margin
    grid_rows = lax.broadcasted_iota(jnp.int32, (height, columns), 0).astype(jnp.float32)
    grid_cols = lax.broadcasted_iota(jnp.int32, (height, columns), 1).astype(jnp.float32)
    place_row = grid_rows + motion[0] + margin
    place_col = grid_cols + motion[1] + margin
    floor_row = jnp.floor(place_row)
    floor_col = jnp.floor(place_col)
    frac_row = place_row - floor_row
    frac_col = place_col - floor_col
    base_index = floor_row.astype(jnp.int32) * stride + floor_col.astype(jnp.int32)
    flat_source = source.reshape(source.shape[0], -1)

    def fetch(step_size):
        picked = jnp.take(flat_source, (base_index + step_size).reshape(-1), axis=1, mode="clip")
        return picked.reshape(source.shape[0], height, columns).astype(jnp.float32)

    blended = (1.0 - frac_row) * (1.0 - frac_col) * fetch(0) + (1.0 - frac_row) * frac_col * fetch(1)
    blended = blended + frac_row * (1.0 - frac_col) * fetch(stride)
    blended = blended + frac_row * frac_col * fetch(stride + 1)
    return blended.astype(jnp.bfloat16)


def reference(features, offsets, fractions, tissue, w_first, w_second, head_weight):
    margin = MAXS + 1
    warped_list = []
    motion_list = []
    for section in range(2):
        own_features = features[section]
        partner = features[1 - section]
        joined = jnp.concatenate([own_features, partner], axis=0)
        padded_joined = jnp.pad(joined, ((0, 0), (1, 1), (1, 1)))
        hidden_one = jax.nn.relu(convolve(padded_joined, w_first, NR, NC)).astype(jnp.bfloat16)
        padded_hidden = jnp.pad(hidden_one, ((0, 0), (1, 1), (1, 1)))
        hidden_two = jax.nn.relu(convolve(padded_hidden, w_second, NR, NC)).astype(jnp.bfloat16)
        residual = jnp.tanh(jnp.dot(head_weight, hidden_two.reshape(C, NR * NC), preferred_element_type=jnp.float32))
        residual = residual.reshape(2, NR, NC)
        coverage = jnp.repeat(jnp.repeat(tissue[section], BLK, axis=0), BLK, axis=1).astype(jnp.float32)
        motion = offsets[section].astype(jnp.float32) + fractions[section].astype(jnp.float32) / frac_scale
        motion = motion + coverage[None] * residual
        banded = jnp.pad(own_features, ((0, 0), (margin, margin), (margin, margin)))
        warped_list.append(sample(banded, motion, margin, NR, NC))
        motion_list.append(motion)
    return jnp.stack(warped_list), jnp.stack(motion_list)
```

```python
import functools

import jax
import jax.numpy as jnp
from jax import lax
from jax.experimental import pallas as pl
from jax.experimental.pallas import tpu as pltpu
from jax.sharding import PartitionSpec as P

MAXS = 8
BLK = 8
CH = 64
HALO = MAXS + 1
LANES = 128
RING = 2 * LANES
PITCH = 2 * HALO
GROUPS = ((0, 7), (7, 9), (9, 16))
frac_scale = 256.0


def lane_iota(shape):
    return lax.broadcasted_iota(jnp.int32, shape, len(shape) - 1)


def pack_kernel(feat_ref, tile_ref, edge_ref, rows_ref):
    channels, height, lanes = feat_ref.shape
    for ch in range(channels):
        rows_ref[pl.ds(ch * height, height), :] = feat_ref[ch].astype(jnp.float32)
    lane = lane_iota((channels, lanes))
    for group, (first, last) in enumerate(GROUPS):
        packed = jnp.zeros((channels, lanes), jnp.float32)
        for row in range(first, last):
            value = rows_ref[pl.ds(row, channels, stride=height), :]
            tile_ref[row] = value.astype(jnp.bfloat16)
            at = PITCH * (row - first)
            turned = pltpu.roll(value, (at + HALO) % lanes, 1)
            packed = jnp.where((lane >= at) & (lane < at + PITCH), turned, packed)
        edge_ref[group] = packed.astype(jnp.bfloat16)


def band_kernel(tile_ref, edge_ref, above_ref, below_ref, band_ref, send_ref):
    height, channels, lanes = tile_ref.shape
    lane = lane_iota((channels, lanes))
    reach = 2
    row_of = []
    for row in range(-HALO, height + HALO):
        if row < 0:
            ref, center, part = above_ref, row + HALO, row + height
            base, groups = HALO, (1, 2)
        elif row < height:
            ref, center, part = tile_ref, row, row
            base, groups = 0, (0, 1, 2)
        else:
            ref, center, part = below_ref, row - height, row - height
            base, groups = HALO, (0, 1)
        group = next(g for g in groups if GROUPS[g][0] <= part < GROUPS[g][1])
        source = edge_ref if ref is tile_ref else ref
        row_of.append((row, ref, center, source, base + groups.index(group), part - GROUPS[group][0]))
    packed = jnp.zeros((channels, lanes), jnp.float32)
    for index, (row, ref, center, source, slot, place) in enumerate(row_of):
        block = pl.ds(index * channels, channels)
        band_ref[block, :lanes] = ref[center]
        at = PITCH * place + HALO
        border = pltpu.roll(source[slot].astype(jnp.float32), (-at) % lanes, 1)
        band_ref[block, lanes:] = border.astype(jnp.bfloat16)
        if -reach <= row < height + reach:
            send_ref[row + reach] = ref[center]
            at = 2 * reach * (row + reach)
            turned = pltpu.roll(border, (at + reach) % lanes, 1)
            packed = jnp.where((lane >= at) & (lane < at + 2 * reach), turned, packed)
    send_ref[height + 2 * reach] = packed.astype(jnp.bfloat16)


def shifted_sum(stacked):
    count = stacked.shape[0] // 3
    left = pltpu.roll(stacked[:count], 1, 1)
    right = pltpu.roll(stacked[2 * count :], RING - 1, 1)
    return left + stacked[count : 2 * count] + right


def main_kernel(
    edges_ref, band_ref, other_ref, own_w_ref, other_w_ref, second_w_ref, head_ref, base_ref, cover_ref,
    warped_ref, motion_ref, window_ref, hidden_ref, residual_ref, rows_ref,
):
    channels, height, lanes = warped_ref.shape
    reach = 2
    window = height + 2 * reach
    border_pack = other_ref[window].astype(jnp.float32)
    for index in range(window):
        block = pl.ds(index * channels, channels)
        window_ref[block, :lanes] = other_ref[index]
        at = 2 * reach * index + reach
        window_ref[block, lanes:] = pltpu.roll(border_pack, (-at) % lanes, 1).astype(jnp.bfloat16)

    lane = lane_iota((1, RING))
    outside = ((edges_ref[2] != 0) & (lane == RING - 1)) | ((edges_ref[3] != 0) & (lane == lanes))
    inside = jnp.where(outside, 0.0, 1.0)
    for row in range(-1, height + 1):
        own = band_ref[pl.ds((row - 1 + HALO) * channels, 3 * channels), :]
        other = window_ref[pl.ds((row - 1 + reach) * channels, 3 * channels), :]
        total = jnp.dot(own_w_ref[...], own, preferred_element_type=jnp.float32)
        total = total + jnp.dot(other_w_ref[...], other, preferred_element_type=jnp.float32)
        keep = inside
        if row == -1:
            keep = jnp.where(edges_ref[0] != 0, 0.0, inside)
        elif row == height:
            keep = jnp.where(edges_ref[1] != 0, 0.0, inside)
        value = jnp.maximum(shifted_sum(total), 0.0) * keep
        hidden_ref[pl.ds((row + 1) * channels, channels), :] = value.astype(jnp.bfloat16)

    for row in range(height):
        taken = hidden_ref[pl.ds(row * channels, 3 * channels), :]
        total = jnp.dot(second_w_ref[...], taken, preferred_element_type=jnp.float32)
        value = jnp.maximum(shifted_sum(total)[:, :lanes], 0.0).astype(jnp.bfloat16)
        pair = jnp.dot(head_ref[...], value, preferred_element_type=jnp.float32)
        for k in range(2):
            residual_ref[k, pl.ds(row, 1), :] = pair[k : k + 1]

    motion = base_ref[...] + cover_ref[...][None] * jnp.tanh(residual_ref[...])
    motion_ref[...] = motion

    at = lax.broadcasted_iota(jnp.int32, (RING, RING), 0)
    column = jnp.where(at < RING - LANES // 2, at, at - RING).astype(jnp.float32)
    grid = (lane & (lanes - 1)).astype(jnp.float32)
    for row in range(0, height, 2):
        move = [jnp.concatenate([motion_ref[k, row : row + 1, :], motion_ref[k, row + 1 : row + 2, :]], axis=1) for k in range(2)]
        place_col = grid + move[1]
        hat = jnp.maximum(1.0 - jnp.abs(place_col - column), 0.0).astype(jnp.bfloat16)
        span = 2 * HALO + 2
        mixed = jnp.dot(band_ref[pl.ds(row * channels, span * channels), :], hat, preferred_element_type=jnp.float32)
        place_row = jnp.where(lane < lanes, 0.0, 1.0) + move[0]
        total = None
        for step in range(span):
            weight = jnp.maximum(1.0 - jnp.abs(place_row - (step - HALO)), 0.0)
            term = weight * mixed[step * channels : (step + 1) * channels]
            total = term if total is None else total + term
        rows_ref[pl.ds(row * channels, channels), :] = total[:, :lanes]
        rows_ref[pl.ds((row + 1) * channels, channels), :] = total[:, lanes:]
    for ch in range(channels):
        warped_ref[ch] = rows_ref[pl.ds(ch, height, stride=channels), :].astype(jnp.bfloat16)


VMEM = pl.BlockSpec(memory_space=pltpu.VMEM)
SMEM = pl.BlockSpec(memory_space=pltpu.SMEM)


def call(body, outputs, scratch, *operands, scalars=0, flops=0):
    moved = sum(x.size * x.dtype.itemsize for x in (*operands, *outputs))
    return pl.pallas_call(
        body,
        out_shape=outputs,
        in_specs=[SMEM] * scalars + [VMEM] * (len(operands) - scalars),
        out_specs=[VMEM] * len(outputs),
        scratch_shapes=scratch,
        compiler_params=pltpu.CompilerParams(vmem_limit_bytes=40 * 2**20),
        cost_estimate=pl.CostEstimate(flops=flops, bytes_accessed=moved, transcendentals=0),
    )(*operands)


def of(shape, dtype=jnp.bfloat16):
    return jax.ShapeDtypeStruct(shape, dtype)


def taps(weights):
    outputs, inputs = weights.shape[1:]
    cube = weights.reshape(3, 3, outputs, inputs).transpose(1, 2, 0, 3)
    return cube.reshape(3 * outputs, 3 * inputs)


def ring(value, axis, step):
    peers = lax.axis_size(axis)
    return lax.ppermute(value, axis, [(i, (i + step) % peers) for i in range(peers)])


def chain(value, axis, step):
    peers = lax.axis_size(axis)
    return lax.ppermute(value, axis, [(i, i + step) for i in range(peers) if 0 <= i + step < peers])


def shards(features, offsets, fractions, tissue, w_first, w_second, head_weight):
    _, channels, height, columns = features.shape
    f32, bf16 = jnp.float32, jnp.bfloat16
    row, col = lax.axis_index("row"), lax.axis_index("col")
    rows, cols = lax.axis_size("row"), lax.axis_size("col")
    edges = jnp.stack([row == 0, row == rows - 1, col == 0, col == cols - 1]).astype(jnp.int32)

    tile, edge = call(
        pack_kernel,
        [of((height, channels, columns)), of((3, channels, columns))],
        [pltpu.VMEM((height * channels, columns), f32)],
        features[0],
    )
    from_left = ring(edge, "col", 1)
    from_right = ring(edge, "col", -1)
    place = jnp.arange(columns) % PITCH
    is_left = place < HALO
    joined = jnp.where(
        is_left,
        jnp.where(col == 0, jnp.zeros_like(from_left), from_left),
        jnp.where(col == cols - 1, jnp.zeros_like(from_right), from_right),
    )
    above = chain(jnp.concatenate([tile[height - HALO :], joined[1:]]), "row", 1)
    below = chain(jnp.concatenate([tile[:HALO], joined[:2]]), "row", -1)
    band_rows = height + 2 * HALO
    band, send = call(
        band_kernel,
        [of((band_rows * channels, RING)), of((height + 5, channels, columns))],
        [],
        tile, joined, above, below,
    )
    other = lax.ppermute(send, "pair", [(0, 1), (1, 0)])

    coverage = jnp.repeat(jnp.repeat(tissue[0], BLK, axis=0), BLK, axis=1).astype(f32)
    base = offsets[0].astype(f32) + fractions[0].astype(f32) / frac_scale
    head = jnp.concatenate([head_weight, jnp.zeros((6, channels), bf16)])
    warped, motion = call(
        main_kernel,
        [of((channels, height, columns)), of((2, height, columns), f32)],
        [
            pltpu.VMEM(((height + 4) * channels, RING), bf16),
            pltpu.VMEM(((height + 2) * channels, RING), bf16),
            pltpu.VMEM((2, height, columns), f32),
            pltpu.VMEM((height * channels, columns), f32),
        ],
        edges, band, other, taps(w_first[:, :, :channels]), taps(w_first[:, :, channels:]), taps(w_second),
        head, base, coverage,
        scalars=1,
    )
    return (warped[None], motion[None])


def solution(mesh):
    return jax.shard_map(
        shards,
        mesh=mesh,
        in_specs=(
            P("pair", None, "row", "col"),
            P("pair", None, "row", "col"),
            P("pair", None, "row", "col"),
            P("pair", "row", "col"),
            P(),
            P(),
            P(),
        ),
        out_specs=(P("pair", None, "row", "col"), P("pair", None, "row", "col")),
        check_vma=False,
    )
```

```python
import functools

import jax
import jax.numpy as jnp
from jax import lax
from jax.experimental import pallas as pl
from jax.experimental.pallas import tpu as pltpu
from jax.sharding import PartitionSpec as P

MAXS = 8
BLK = 8
CH = 64
HALO = MAXS + 1
LANES = 128
RING = 2 * LANES
PITCH = 2 * HALO
GROUPS = ((0, 7), (7, 9), (9, 16))
frac_scale = 256.0


def lane_iota(shape):
    return lax.broadcasted_iota(jnp.int32, shape, len(shape) - 1)


def packed_edge(value, slot):
    return pltpu.roll(value, (PITCH * slot + HALO) % LANES, 1)


def in_slot(lane, slot):
    return (lane >= PITCH * slot) & (lane < PITCH * (slot + 1))


def border_of(vector, slot):
    return pltpu.roll(vector, (-PITCH * slot - HALO) % LANES, 1)


def own_pack_kernel(feat_ref, tile_ref, edge_ref, rows_ref):
    channels, height, lanes = feat_ref.shape
    for ch in range(channels):
        rows_ref[pl.ds(ch * height, height), :] = feat_ref[ch].astype(jnp.float32)
    lane = lane_iota((channels, lanes))
    for group, (first, last) in enumerate(GROUPS):
        packed = jnp.zeros((channels, lanes), jnp.float32)
        for row in range(first, last):
            value = rows_ref[pl.ds(row, channels, stride=height), :]
            tile_ref[row] = value.astype(jnp.bfloat16)
            packed = jnp.where(in_slot(lane, row - first), packed_edge(value, row - first), packed)
        edge_ref[group] = packed.astype(jnp.bfloat16)


def other_pack_kernel(feat_ref, own_tile_ref, own_edge_ref, tile_ref, edge_ref, rows_ref):
    channels, height, lanes = feat_ref.shape
    edge_ref[: len(GROUPS)] = own_edge_ref[...]
    own_pack_kernel(feat_ref, tile_ref, edge_ref.at[pl.ds(len(GROUPS), len(GROUPS))], rows_ref)
    lane = lane_iota((channels, lanes))
    packed = edge_ref[len(GROUPS) + 1].astype(jnp.float32)
    for slot, row in enumerate((0, 1, height - 2, height - 1), 2):
        value = own_tile_ref[row].astype(jnp.float32)
        packed = jnp.where(in_slot(lane, slot), packed_edge(value, slot), packed)
    edge_ref[len(GROUPS) + 1] = packed.astype(jnp.bfloat16)


def lay(target_ref, index, center, vector, slot):
    channels, lanes = center.shape
    block = pl.ds(index * channels, channels)
    target_ref[block, :lanes] = center
    target_ref[block, lanes:] = border_of(vector, slot).astype(jnp.bfloat16)


def hidden_row(own, other, own_w_ref, other_w_ref, keep):
    total = jnp.dot(own_w_ref[...], own, preferred_element_type=jnp.float32)
    total = total + jnp.dot(other_w_ref[...], other, preferred_element_type=jnp.float32)
    return (jnp.maximum(shifted_sum(total), 0.0) * keep).astype(jnp.bfloat16)


def residual_row(taken, second_w_ref, head_ref):
    total = jnp.dot(second_w_ref[...], taken, preferred_element_type=jnp.float32)
    value = jnp.maximum(shifted_sum(total)[:, :LANES], 0.0).astype(jnp.bfloat16)
    return jnp.dot(head_ref[...], value, preferred_element_type=jnp.float32)


def inside_columns(edges_ref):
    lane = lane_iota((1, RING))
    outside = ((edges_ref[2] != 0) & (lane == RING - 1)) | ((edges_ref[3] != 0) & (lane == LANES))
    return jnp.where(outside, 0.0, 1.0)


def middle_kernel(
    edges_ref, own_tile_ref, other_tile_ref, joined_ref, own_w_ref, other_w_ref, second_w_ref, head_ref,
    band_ref, window_ref, near_ref, residual_ref, hidden_ref,
):
    height, channels, lanes = own_tile_ref.shape
    for part, (tile_ref, target_ref) in enumerate(((own_tile_ref, band_ref), (other_tile_ref, window_ref))):
        for group, (first, last) in enumerate(GROUPS):
            vector = joined_ref[part * len(GROUPS) + group].astype(jnp.float32)
            for row in range(first, last):
                lay(target_ref, row, tile_ref[row], vector, row - first)
    keep = inside_columns(edges_ref)
    for row in range(1, height - 1):
        block = pl.ds((row - 1) * channels, 3 * channels)
        value = hidden_row(band_ref[block, :], window_ref[block, :], own_w_ref, other_w_ref, keep)
        hidden_ref[pl.ds((row - 1) * channels, channels), :] = value
    near_ref[: 2 * channels] = hidden_ref[: 2 * channels]
    near_ref[2 * channels :] = hidden_ref[(height - 4) * channels :]
    for row in range(2, height - 2):
        pair = residual_row(hidden_ref[pl.ds((row - 2) * channels, 3 * channels), :], second_w_ref, head_ref)
        for k in range(2):
            residual_ref[k, pl.ds(row, 1), :] = pair[k : k + 1]
    for row in (0, 1, height - 2, height - 1):
        for k in range(2):
            residual_ref[k, pl.ds(row, 1), :] = jnp.zeros((1, lanes), jnp.float32)


def shifted_sum(stacked):
    count = stacked.shape[0] // 3
    left = pltpu.roll(stacked[:count], 1, 1)
    right = pltpu.roll(stacked[2 * count :], RING - 1, 1)
    return left + stacked[count : 2 * count] + right


def last_kernel(
    edges_ref, inner_ref, window_ref, near_ref, part_ref, above_ref, below_ref,
    own_w_ref, other_w_ref, second_w_ref, head_ref, base_ref, cover_ref,
    warped_ref, motion_ref, band_ref, side_ref, hidden_ref, residual_ref, rows_ref,
):
    channels, height, lanes = warped_ref.shape
    start, stop = HALO * channels, (HALO + height) * channels
    band_ref[start:stop, :] = inner_ref[...]
    first, middle = (above_ref[HALO + 3].astype(jnp.float32), above_ref[HALO + 2].astype(jnp.float32))
    for index in range(HALO):
        lay(band_ref, index, above_ref[index], *((middle, index) if index < 2 else (first, index - 2)))
    lay(side_ref, 0, above_ref[HALO], middle, 4)
    lay(side_ref, 1, above_ref[HALO + 1], middle, 5)
    first, middle = (below_ref[HALO + 2].astype(jnp.float32), below_ref[HALO + 3].astype(jnp.float32))
    for index in range(HALO):
        lay(band_ref, HALO + height + index, below_ref[index], *((first, index) if index < 7 else (middle, index - 7)))
    lay(side_ref, 6, below_ref[HALO], middle, 2)
    lay(side_ref, 7, below_ref[HALO + 1], middle, 3)
    half = 2 * channels
    for side, at in ((0, 0), (4, height - 2)):
        side_ref[pl.ds((side + 2 if side == 0 else side) * channels, half), :] = window_ref[pl.ds(at * channels, half), :]
    hidden_ref[half : 2 * half, :] = near_ref[:half, :]
    hidden_ref[2 * half : 3 * half, :] = near_ref[half:, :]
    inside = inside_columns(edges_ref)
    for row, side, spot in ((-1, 0, 0), (0, 1, 1), (height - 1, 4, 6), (height, 5, 7)):
        own = band_ref[pl.ds((row - 1 + HALO) * channels, 3 * channels), :]
        other = side_ref[pl.ds(side * channels, 3 * channels), :]
        keep = inside
        if row == -1:
            keep = jnp.where(edges_ref[0] != 0, 0.0, inside)
        elif row == height:
            keep = jnp.where(edges_ref[1] != 0, 0.0, inside)
        hidden_ref[pl.ds(spot * channels, channels), :] = hidden_row(own, other, own_w_ref, other_w_ref, keep)
    residual_ref[...] = part_ref[...]
    for row, spot in ((0, 0), (1, 1), (height - 2, 4), (height - 1, 5)):
        pair = residual_row(hidden_ref[pl.ds(spot * channels, 3 * channels), :], second_w_ref, head_ref)
        for k in range(2):
            residual_ref[k, pl.ds(row, 1), :] = pair[k : k + 1]

    motion = base_ref[...] + cover_ref[...][None] * jnp.tanh(residual_ref[...])
    motion_ref[...] = motion
    lane = lane_iota((1, RING))

    at = lax.broadcasted_iota(jnp.int32, (RING, RING), 0)
    column = jnp.where(at < RING - LANES // 2, at, at - RING).astype(jnp.float32)
    grid = (lane & (lanes - 1)).astype(jnp.float32)
    for row in range(0, height, 2):
        move = [jnp.concatenate([motion_ref[k, row : row + 1, :], motion_ref[k, row + 1 : row + 2, :]], axis=1) for k in range(2)]
        place_col = grid + move[1]
        hat = jnp.maximum(1.0 - jnp.abs(place_col - column), 0.0).astype(jnp.bfloat16)
        span = 2 * HALO + 2
        mixed = jnp.dot(band_ref[pl.ds(row * channels, span * channels), :], hat, preferred_element_type=jnp.float32)
        place_row = jnp.where(lane < lanes, 0.0, 1.0) + move[0]
        total = None
        for step in range(span):
            weight = jnp.maximum(1.0 - jnp.abs(place_row - (step - HALO)), 0.0)
            term = weight * mixed[step * channels : (step + 1) * channels]
            total = term if total is None else total + term
        rows_ref[pl.ds(row * channels, channels), :] = total[:, :lanes]
        rows_ref[pl.ds((row + 1) * channels, channels), :] = total[:, lanes:]
    for ch in range(channels):
        warped_ref[ch] = rows_ref[pl.ds(ch, height, stride=channels), :].astype(jnp.bfloat16)


VMEM = pl.BlockSpec(memory_space=pltpu.VMEM)
SMEM = pl.BlockSpec(memory_space=pltpu.SMEM)


def call(body, outputs, scratch, *operands, scalars=0, flops=0):
    moved = sum(x.size * x.dtype.itemsize for x in (*operands, *outputs))
    return pl.pallas_call(
        body,
        out_shape=outputs,
        in_specs=[SMEM] * scalars + [VMEM] * (len(operands) - scalars),
        out_specs=[VMEM] * len(outputs),
        scratch_shapes=scratch,
        compiler_params=pltpu.CompilerParams(vmem_limit_bytes=40 * 2**20),
        cost_estimate=pl.CostEstimate(flops=flops, bytes_accessed=moved, transcendentals=0),
    )(*operands)


def of(shape, dtype=jnp.bfloat16):
    return jax.ShapeDtypeStruct(shape, dtype)


def taps(weights):
    outputs, inputs = weights.shape[1:]
    cube = weights.reshape(3, 3, outputs, inputs).transpose(1, 2, 0, 3)
    return cube.reshape(3 * outputs, 3 * inputs)


def ring(value, axis, step):
    peers = lax.axis_size(axis)
    return lax.ppermute(value, axis, [(i, (i + step) % peers) for i in range(peers)])


def across(value, step):
    rows, cols = lax.axis_size("row"), lax.axis_size("col")
    place = lambda pair, row, col: (pair * rows + row) * cols + col
    pairs = [
        (place(pair, row, col), place(1 - pair, row + step, col))
        for pair in range(2)
        for row in range(rows)
        if 0 <= row + step < rows
        for col in range(cols)
    ]
    return lax.ppermute(value, ("pair", "row", "col"), pairs)


def shards(features, offsets, fractions, tissue, w_first, w_second, head_weight):
    _, channels, height, columns = features.shape
    f32, bf16 = jnp.float32, jnp.bfloat16
    row, col = lax.axis_index("row"), lax.axis_index("col")
    rows, cols = lax.axis_size("row"), lax.axis_size("col")
    edges = jnp.stack([row == 0, row == rows - 1, col == 0, col == cols - 1]).astype(jnp.int32)

    partner = lax.ppermute(features[0], "pair", [(0, 1), (1, 0)])
    tile_shape = (height, channels, columns)
    scratch = [pltpu.VMEM((height * channels, columns), f32)]
    own_tile, own_edge = call(own_pack_kernel, [of(tile_shape), of((3, channels, columns))], scratch, features[0])
    other_tile, edge = call(
        other_pack_kernel, [of(tile_shape), of((6, channels, columns))], scratch, partner, own_tile, own_edge
    )
    from_left = ring(edge, "col", 1)
    from_right = ring(edge, "col", -1)
    is_left = jnp.arange(columns) % PITCH < HALO
    joined = jnp.where(
        is_left,
        jnp.where(col == 0, jnp.zeros_like(from_left), from_left),
        jnp.where(col == cols - 1, jnp.zeros_like(from_right), from_right),
    )
    above = across(jnp.concatenate([other_tile[height - HALO :], own_tile[height - 2 :], joined[4:6]]), 1)
    below = across(jnp.concatenate([other_tile[:HALO], own_tile[:2], joined[3:5]]), -1)

    coverage = jnp.repeat(jnp.repeat(tissue[0], BLK, axis=0), BLK, axis=1).astype(f32)
    base = offsets[0].astype(f32) + fractions[0].astype(f32) / frac_scale
    weights = (
        taps(w_first[:, :, :channels]),
        taps(w_first[:, :, channels:]),
        taps(w_second),
        jnp.concatenate([head_weight, jnp.zeros((6, channels), bf16)]),
    )
    inner, window, near, part = call(
        middle_kernel,
        [
            of((height * channels, RING)),
            of((height * channels, RING)),
            of((4 * channels, RING)),
            of((2, height, columns), f32),
        ],
        [pltpu.VMEM(((height - 2) * channels, RING), bf16)],
        edges, own_tile, other_tile, joined, *weights,
        scalars=1, flops=3 * 10**9,
    )
    warped, motion = call(
        last_kernel,
        [of((channels, height, columns)), of((2, height, columns), f32)],
        [
            pltpu.VMEM(((height + 2 * HALO) * channels, RING), bf16),
            pltpu.VMEM((8 * channels, RING), bf16),
            pltpu.VMEM((8 * channels, RING), bf16),
            pltpu.VMEM((2, height, columns), f32),
            pltpu.VMEM((height * channels, columns), f32),
        ],
        edges, inner, window, near, part, above, below, *weights, base, coverage,
        scalars=1, flops=3 * 10**9,
    )
    return (warped[None], motion[None])


def solution(mesh):
    return jax.shard_map(
        shards,
        mesh=mesh,
        in_specs=(
            P("pair", None, "row", "col"),
            P("pair", None, "row", "col"),
            P("pair", None, "row", "col"),
            P("pair", "row", "col"),
            P(),
            P(),
            P(),
        ),
        out_specs=(P("pair", None, "row", "col"), P("pair", None, "row", "col")),
        check_vma=False,
    )
```

```python
import functools

import jax
import jax.numpy as jnp
from jax import lax
from jax.experimental import pallas as pl
from jax.experimental.pallas import tpu as pltpu
from jax.sharding import PartitionSpec as P

MAXS = 8
BLK = 8
CH = 64
HALO = MAXS + 1
LANES = 128
RING = 2 * LANES
PITCH = 2 * HALO
GROUPS = ((0, 7), (7, 9), (9, 16))


def EXTRA(height):
    return [0, 1, height - 2, height - 1]


frac_scale = 256.0


def lane_iota(shape):
    return lax.broadcasted_iota(jnp.int32, shape, len(shape) - 1)


def packed_edge(value, slot):
    return pltpu.roll(value, (PITCH * slot + HALO) % LANES, 1)


def in_slot(lane, slot):
    return (lane >= PITCH * slot) & (lane < PITCH * (slot + 1))


def border_of(vector, slot):
    return pltpu.roll(vector, (-PITCH * slot - HALO) % LANES, 1)


def pack_kernel(feat_ref, tile_ref, edge_ref, rows_ref):
    channels, height, lanes = feat_ref.shape
    for ch in range(channels):
        rows_ref[pl.ds(ch * height, height), :] = feat_ref[ch].astype(jnp.float32)
    lane = lane_iota((channels, lanes))
    for group, (first, last) in enumerate(GROUPS):
        packed = jnp.zeros((channels, lanes), jnp.float32)
        taken = list(range(first, last))
        if group == 1:
            taken += EXTRA(height)
        for slot, row in enumerate(taken):
            value = rows_ref[pl.ds(row, channels, stride=height), :]
            if slot < last - first:
                tile_ref[row] = value.astype(jnp.bfloat16)
            packed = jnp.where(in_slot(lane, slot), packed_edge(value, slot), packed)
        edge_ref[group] = packed.astype(jnp.bfloat16)


def shifted_sum(stacked):
    count = stacked.shape[0] // 3
    left = pltpu.roll(stacked[:count], 1, 1)
    right = pltpu.roll(stacked[2 * count :], RING - 1, 1)
    return left + stacked[count : 2 * count] + right


def transpose_kernel(feat_ref, tile_ref, rows_ref):
    channels, height, _ = feat_ref.shape
    for ch in range(channels):
        rows_ref[pl.ds(ch * height, height), :] = feat_ref[ch].astype(jnp.float32)
    for row in range(height):
        tile_ref[row] = rows_ref[pl.ds(row, channels, stride=height), :].astype(jnp.bfloat16)


def hidden_row(taken, first_w_ref, keep):
    total = jnp.dot(first_w_ref[...], taken, preferred_element_type=jnp.float32)
    return (jnp.maximum(shifted_sum(total), 0.0) * keep).astype(jnp.bfloat16)


def residual_row(taken, second_w_ref, head_ref):
    total = jnp.dot(second_w_ref[...], taken, preferred_element_type=jnp.float32)
    value = jnp.maximum(shifted_sum(total)[:, :LANES], 0.0).astype(jnp.bfloat16)
    return jnp.dot(head_ref[...], value, preferred_element_type=jnp.float32)


def inside_columns(edges_ref):
    lane = lane_iota((1, RING))
    outside = ((edges_ref[2] != 0) & (lane == RING - 1)) | ((edges_ref[3] != 0) & (lane == LANES))
    return jnp.where(outside, 0.0, 1.0)


def two_rows(motion_ref, k, row):
    return jnp.concatenate([motion_ref[k, row : row + 1, :], motion_ref[k, row + 1 : row + 2, :]], axis=1)


def column_weights(motion_ref, row):
    at = lax.broadcasted_iota(jnp.int32, (RING, RING), 0)
    column = jnp.where(at < RING - LANES // 2, at, at - RING).astype(jnp.float32)
    place = (lane_iota((1, RING)) & (LANES - 1)).astype(jnp.float32) + two_rows(motion_ref, 1, row)
    return jnp.maximum(1.0 - jnp.abs(place - column), 0.0).astype(jnp.bfloat16)


def warp_part(motion_ref, row, hat, source, first, count, total):
    mixed = jnp.dot(source, hat, preferred_element_type=jnp.float32)
    place = jnp.where(lane_iota((1, RING)) < LANES, 0.0, 1.0) + two_rows(motion_ref, 0, row)
    channels = source.shape[0] // count
    for step in range(count):
        weight = jnp.maximum(1.0 - jnp.abs(place - (first + step - row)), 0.0)
        term = weight * mixed[step * channels : (step + 1) * channels]
        total = term if total is None else total + term
    return total


def lay_both(tile, vector, slot, *targets):
    border = border_of(vector, slot).astype(jnp.bfloat16)
    for ref, start in targets:
        block = pl.ds(start, tile.shape[0])
        ref[block, :LANES] = tile
        ref[block, LANES:] = border


def middle_kernel(
    edges_ref, own_tile_ref, other_tile_ref, own_joined_ref, other_joined_ref,
    w_first_ref, w_second_ref, head_ref, offsets_ref, fractions_ref, tissue_ref,
    band_ref, side_ref, near_ref, part_ref, base_ref, cover_ref, first_w_ref, second_w_ref, sums_ref,
    window_ref, hidden_ref, motion_ref,
):
    height, channels, lanes = own_tile_ref.shape
    both = 2 * channels
    for b in range(3):
        block = pl.ds(b * channels, channels)
        for a in range(3):
            first_w_ref[block, a * both : (a + 1) * both] = w_first_ref[3 * a + b]
        second_w_ref[block, :both] = jnp.concatenate([w_second_ref[b], w_second_ref[3 + b]], axis=1)
        second_w_ref[block, both:] = w_second_ref[6 + b]
    for group, (first, last) in enumerate(GROUPS):
        own_vector = own_joined_ref[group].astype(jnp.float32)
        other_vector = other_joined_ref[group].astype(jnp.float32)
        for row in range(first, last):
            lay_both(own_tile_ref[row], own_vector, row - first, (band_ref, row * channels), (window_ref, row * both))
            lay_both(other_tile_ref[row], other_vector, row - first, (window_ref, row * both + channels))
    side_ref[: 2 * both] = window_ref[: 2 * both]
    side_ref[2 * both :] = window_ref[(height - 2) * both :]
    keep = inside_columns(edges_ref)
    for row in range(1, height - 1):
        taken = window_ref[pl.ds((row - 1) * both, 3 * both), :]
        hidden_ref[pl.ds((row - 1) * channels, channels), :] = hidden_row(taken, first_w_ref, keep)
    near_ref[:both] = hidden_ref[:both]
    near_ref[both:] = hidden_ref[(height - 4) * channels :]
    part_ref[...] = jnp.zeros_like(part_ref)
    for row in range(2, height - 2):
        pair = residual_row(hidden_ref[pl.ds((row - 2) * channels, 3 * channels), :], second_w_ref, head_ref)
        for k in range(2):
            part_ref[k, pl.ds(row, 1), :] = pair[k : k + 1]

    cells = tissue_ref[...].astype(jnp.float32)
    count = cells.shape[1]
    spread = lax.broadcasted_iota(jnp.int32, (count, lanes), 1) // BLK == lax.broadcasted_iota(jnp.int32, (count, lanes), 0)
    spread = jnp.dot(cells, spread.astype(jnp.float32), preferred_element_type=jnp.float32)
    for cell in range(cells.shape[0]):
        cover_ref[pl.ds(cell * BLK, BLK), :] = jnp.broadcast_to(spread[cell : cell + 1], (BLK, lanes))
    base_ref[...] = offsets_ref[...].astype(jnp.float32) + fractions_ref[...].astype(jnp.float32) / frac_scale
    motion_ref[...] = base_ref[...] + cover_ref[...][None] * jnp.tanh(part_ref[...])
    for row in range(2, height - 2, 2):
        first, last = max(0, row - HALO), min(height, row + HALO + 2)
        source = band_ref[pl.ds(first * channels, (last - first) * channels), :]
        hat = column_weights(motion_ref, row)
        sums_ref[pl.ds((row // 2 - 1) * channels, channels), :] = warp_part(
            motion_ref, row, hat, source, first, last - first, None
        )


def last_kernel(
    edges_ref, inner_ref, near_side_ref, near_ref, part_ref, base_ref, cover_ref, first_w_ref, second_w_ref, sums_ref,
    above_ref, below_ref, head_ref,
    warped_ref, motion_ref, band_ref, side_ref, hidden_ref, residual_ref, rows_ref,
):
    channels, height, lanes = warped_ref.shape
    both = 2 * channels
    start, stop = HALO * channels, (HALO + height) * channels
    band_ref[start:stop, :] = inner_ref[...]
    side_ref[2 * both : 4 * both, :] = near_side_ref[: 2 * both, :]
    side_ref[4 * both : 6 * both, :] = near_side_ref[2 * both :, :]
    middle, last = above_ref[HALO + 2].astype(jnp.float32), above_ref[HALO + 3].astype(jnp.float32)
    for index in range(HALO):
        targets = [(band_ref, index * channels)]
        if index >= HALO - 2:
            targets.append((side_ref, (index - HALO + 2) * both))
        lay_both(above_ref[index], *((middle, index) if index < 2 else (last, index - 2)), *targets)
    first, center = below_ref[HALO + 2].astype(jnp.float32), below_ref[HALO + 3].astype(jnp.float32)
    for index in range(HALO):
        targets = [(band_ref, stop + index * channels)]
        if index < 2:
            targets.append((side_ref, (6 + index) * both))
        lay_both(below_ref[index], *((first, index) if index < 7 else (center, index - 7)), *targets)
    for index in range(2):
        lay_both(above_ref[HALO + index], middle, 4 + index, (side_ref, index * both + channels))
        lay_both(below_ref[HALO + index], center, 2 + index, (side_ref, (6 + index) * both + channels))
    hidden_ref[both : 2 * both, :] = near_ref[:both, :]
    hidden_ref[2 * both : 3 * both, :] = near_ref[both:, :]
    inside = inside_columns(edges_ref)
    for row, side, spot in ((-1, 0, 0), (0, 1, 1), (height - 1, 4, 6), (height, 5, 7)):
        keep = inside
        if row == -1:
            keep = jnp.where(edges_ref[0] != 0, 0.0, inside)
        elif row == height:
            keep = jnp.where(edges_ref[1] != 0, 0.0, inside)
        taken = side_ref[pl.ds(side * both, 3 * both), :]
        hidden_ref[pl.ds(spot * channels, channels), :] = hidden_row(taken, first_w_ref, keep)
    residual_ref[...] = part_ref[...]
    for row, spot in ((0, 0), (1, 1), (height - 2, 4), (height - 1, 5)):
        pair = residual_row(hidden_ref[pl.ds(spot * channels, 3 * channels), :], second_w_ref, head_ref)
        for k in range(2):
            residual_ref[k, pl.ds(row, 1), :] = pair[k : k + 1]
    motion_ref[...] = base_ref[...] + cover_ref[...][None] * jnp.tanh(residual_ref[...])

    for row in range(0, height, 2):
        low, high = row - HALO, row + HALO + 2
        if 2 <= row < height - 2:
            total = sums_ref[pl.ds((row // 2 - 1) * channels, channels), :]
            spans = [(low, min(high, 0)), (max(low, height), high)]
        else:
            total = None
            spans = [(low, high)]
        hat = column_weights(motion_ref, row)
        for first, last in spans:
            if first < last:
                source = band_ref[pl.ds((first + HALO) * channels, (last - first) * channels), :]
                total = warp_part(motion_ref, row, hat, source, first, last - first, total)
        rows_ref[pl.ds(row * channels, channels), :] = total[:, :lanes]
        rows_ref[pl.ds((row + 1) * channels, channels), :] = total[:, lanes:]
    for ch in range(channels):
        warped_ref[ch] = rows_ref[pl.ds(ch, height, stride=channels), :].astype(jnp.bfloat16)


VMEM = pl.BlockSpec(memory_space=pltpu.VMEM)
SMEM = pl.BlockSpec(memory_space=pltpu.SMEM)


def call(body, outputs, scratch, *operands, scalars=0, flops=0):
    moved = sum(x.size * x.dtype.itemsize for x in (*operands, *outputs))
    return pl.pallas_call(
        body,
        out_shape=outputs,
        in_specs=[SMEM] * scalars + [VMEM] * (len(operands) - scalars),
        out_specs=[VMEM] * len(outputs),
        scratch_shapes=scratch,
        compiler_params=pltpu.CompilerParams(vmem_limit_bytes=40 * 2**20),
        cost_estimate=pl.CostEstimate(flops=flops, bytes_accessed=moved, transcendentals=0),
    )(*operands)


def of(shape, dtype=jnp.bfloat16):
    return jax.ShapeDtypeStruct(shape, dtype)


def ring(value, axis, step):
    peers = lax.axis_size(axis)
    return lax.ppermute(value, axis, [(i, (i + step) % peers) for i in range(peers)])


def across(value, step):
    rows, cols = lax.axis_size("row"), lax.axis_size("col")
    place = lambda pair, row, col: (pair * rows + row) * cols + col
    pairs = [
        (place(pair, row, col), place(1 - pair, row + step, col))
        for pair in range(2)
        for row in range(rows)
        if 0 <= row + step < rows
        for col in range(cols)
    ]
    return lax.ppermute(value, ("pair", "row", "col"), pairs)


def shards(features, offsets, fractions, tissue, w_first, w_second, head_weight):
    _, channels, height, columns = features.shape
    f32, bf16 = jnp.float32, jnp.bfloat16
    row, col = lax.axis_index("row"), lax.axis_index("col")
    rows, cols = lax.axis_size("row"), lax.axis_size("col")
    edges = jnp.stack([row == 0, row == rows - 1, col == 0, col == cols - 1]).astype(jnp.int32)

    swap = [(0, 1), (1, 0)]
    partner = lax.ppermute(features[0], "pair", swap)
    tile_shape = (height, channels, columns)
    scratch = [pltpu.VMEM((height * channels, columns), f32)]
    own_tile, edge = call(pack_kernel, [of(tile_shape), of((3, channels, columns))], scratch, features[0])
    from_left = ring(edge, "col", 1)
    from_right = ring(edge, "col", -1)
    lane = jnp.arange(columns)
    joined = jnp.where(
        lane % PITCH < HALO,
        jnp.where(col == 0, jnp.zeros_like(from_left), from_left),
        jnp.where(col == cols - 1, jnp.zeros_like(from_right), from_right),
    )
    other_joined = lax.ppermute(joined, "pair", swap)
    (other_tile,) = call(transpose_kernel, [of(tile_shape)], scratch, partner)
    mixed = jnp.where(lane < 2 * PITCH, other_joined[1], joined[1])[None]
    above = across(jnp.concatenate([other_tile[height - HALO :], own_tile[height - 2 :], mixed, other_joined[2:]]), 1)
    below = across(jnp.concatenate([other_tile[:HALO], own_tile[:2], other_joined[:1], mixed]), -1)

    wide = height * channels
    middle = call(
        middle_kernel,
        [
            of((wide, RING)),
            of((8 * channels, RING)),
            of((4 * channels, RING)),
            of((2, height, columns), f32),
            of((2, height, columns), f32),
            of((height, columns), f32),
            of((3 * channels, 6 * channels)),
            of((3 * channels, 3 * channels)),
            of(((height // 2 - 2) * channels, RING), f32),
        ],
        [
            pltpu.VMEM((2 * wide, RING), bf16),
            pltpu.VMEM(((height - 2) * channels, RING), bf16),
            pltpu.VMEM((2, height, columns), f32),
        ],
        edges, own_tile, other_tile, joined, other_joined,
        w_first, w_second, head_weight, offsets[0], fractions[0], tissue[0],
        scalars=1, flops=4 * 10**9,
    )
    warped, motion = call(
        last_kernel,
        [of((channels, height, columns)), of((2, height, columns), f32)],
        [
            pltpu.VMEM(((height + 2 * HALO) * channels, RING), bf16),
            pltpu.VMEM((16 * channels, RING), bf16),
            pltpu.VMEM((8 * channels, RING), bf16),
            pltpu.VMEM((2, height, columns), f32),
            pltpu.VMEM((wide, columns), f32),
        ],
        edges, *middle, above, below, head_weight,
        scalars=1, flops=2 * 10**9,
    )
    return (warped[None], motion[None])


def solution(mesh):
    return jax.shard_map(
        shards,
        mesh=mesh,
        in_specs=(
            P("pair", None, "row", "col"),
            P("pair", None, "row", "col"),
            P("pair", None, "row", "col"),
            P("pair", "row", "col"),
            P(),
            P(),
            P(),
        ),
        out_specs=(P("pair", None, "row", "col"), P("pair", None, "row", "col")),
        check_vma=False,
    )
```

```python
import functools

import jax
import jax.numpy as jnp
from jax import lax
from jax.experimental import pallas as pl
from jax.experimental.pallas import tpu as pltpu
from jax.sharding import PartitionSpec as P

MAXS = 8
BLK = 8
CH = 64
HALO = MAXS + 1
LANES = 128
RING = 2 * LANES
PITCH = 2 * HALO
GROUPS = ((0, 7), (7, 9), (9, 16))


def EXTRA(height):
    return [0, 1, height - 2, height - 1]


frac_scale = 256.0


def lane_iota(shape):
    return lax.broadcasted_iota(jnp.int32, shape, len(shape) - 1)


def packed_edge(value, slot):
    return pltpu.roll(value, (PITCH * slot + HALO) % LANES, 1)


def in_slot(lane, slot):
    return (lane >= PITCH * slot) & (lane < PITCH * (slot + 1))


def border_of(vector, slot):
    return pltpu.roll(vector, (-PITCH * slot - HALO) % LANES, 1)


def pack_kernel(feat_ref, tile_ref, edge_ref, rows_ref):
    channels, height, lanes = feat_ref.shape
    for ch in range(channels):
        rows_ref[pl.ds(ch * height, height), :] = feat_ref[ch].astype(jnp.float32)
    lane = lane_iota((channels, lanes))
    for group, (first, last) in enumerate(GROUPS):
        packed = jnp.zeros((channels, lanes), jnp.float32)
        taken = list(range(first, last))
        if group == 1:
            taken += EXTRA(height)
        for slot, row in enumerate(taken):
            value = rows_ref[pl.ds(row, channels, stride=height), :]
            if slot < last - first:
                tile_ref[row] = value.astype(jnp.bfloat16)
            packed = jnp.where(in_slot(lane, slot), packed_edge(value, slot), packed)
        edge_ref[group] = packed.astype(jnp.bfloat16)


def shifted_sum(stacked):
    count = stacked.shape[0] // 3
    left = pltpu.roll(stacked[:count], 1, 1)
    right = pltpu.roll(stacked[2 * count :], RING - 1, 1)
    return left + stacked[count : 2 * count] + right


def transpose_kernel(feat_ref, tile_ref, rows_ref):
    channels, height, _ = feat_ref.shape
    for ch in range(channels):
        rows_ref[pl.ds(ch * height, height), :] = feat_ref[ch].astype(jnp.float32)
    for row in range(height):
        tile_ref[row] = rows_ref[pl.ds(row, channels, stride=height), :].astype(jnp.bfloat16)


def hidden_row(taken, first_w_ref, keep):
    total = jnp.dot(first_w_ref[...], taken, preferred_element_type=jnp.float32)
    return (jnp.maximum(shifted_sum(total), 0.0) * keep).astype(jnp.bfloat16)


def second_row(taken, second_w_ref):
    total = jnp.dot(second_w_ref[...], taken, preferred_element_type=jnp.float32)
    return jnp.maximum(shifted_sum(total)[:, :LANES], 0.0).astype(jnp.bfloat16)


def project(second_ref, rows, head_ref, residual_ref):
    pairs = jnp.dot(head_ref[...], second_ref[...], preferred_element_type=jnp.float32)
    for index, row in enumerate(rows):
        for k in range(2):
            residual_ref[k, pl.ds(row, 1), :] = pairs[k : k + 1, index * LANES : (index + 1) * LANES]


def two_rows(motion_ref, k, row):
    return jnp.concatenate([motion_ref[k, row : row + 1, :], motion_ref[k, row + 1 : row + 2, :]], axis=1)


def column_weights(motion_ref, row):
    place = (lane_iota((1, RING)) & (LANES - 1)).astype(jnp.float32) + two_rows(motion_ref, 1, row)
    parts = []
    for first, count in ((0, LANES + 16), (-16, 16)):
        column = (lax.broadcasted_iota(jnp.int32, (count, RING), 0) + first).astype(jnp.float32)
        parts.append(jnp.maximum(1.0 - jnp.abs(place - column), 0.0).astype(jnp.bfloat16))
    return jnp.concatenate([parts[0], jnp.zeros((RING - LANES - 32, RING), jnp.bfloat16), parts[1]])


def warp_part(motion_ref, row, hat, source, first, count, total):
    mixed = jnp.dot(source, hat, preferred_element_type=jnp.float32)
    place = jnp.where(lane_iota((1, RING)) < LANES, 0.0, 1.0) + two_rows(motion_ref, 0, row)
    channels = source.shape[0] // count
    for step in range(count):
        weight = jnp.maximum(1.0 - jnp.abs(place - (first + step - row)), 0.0)
        term = weight * mixed[step * channels : (step + 1) * channels]
        total = term if total is None else total + term
    return total


def lay_both(tile, vector, slot, *targets):
    border = border_of(vector, slot).astype(jnp.bfloat16)
    for ref, start in targets:
        block = pl.ds(start, tile.shape[0])
        ref[block, :LANES] = tile
        ref[block, LANES:] = border


def middle_kernel(
    keep_ref, own_tile_ref, other_tile_ref, own_joined_ref, other_joined_ref,
    w_first_ref, w_second_ref, head_ref, offsets_ref, fractions_ref, tissue_ref,
    band_ref, side_ref, near_ref, base_ref, cover_ref, first_w_ref, second_w_ref, sums_ref, motion_ref, hats_ref,
    window_ref, hidden_ref, second_ref, part_ref,
):
    height, channels, lanes = own_tile_ref.shape
    both = 2 * channels
    for b in range(3):
        block = pl.ds(b * channels, channels)
        for a in range(3):
            first_w_ref[block, a * both : (a + 1) * both] = w_first_ref[3 * a + b]
        second_w_ref[block, :both] = jnp.concatenate([w_second_ref[b], w_second_ref[3 + b]], axis=1)
        second_w_ref[block, both:] = w_second_ref[6 + b]
    for group, (first, last) in enumerate(GROUPS):
        own_vector = own_joined_ref[group].astype(jnp.float32)
        other_vector = other_joined_ref[group].astype(jnp.float32)
        for row in range(first, last):
            lay_both(own_tile_ref[row], own_vector, row - first, (band_ref, row * channels), (window_ref, row * both))
            lay_both(other_tile_ref[row], other_vector, row - first, (window_ref, row * both + channels))
    side_ref[: 2 * both] = window_ref[: 2 * both]
    side_ref[2 * both :] = window_ref[(height - 2) * both :]
    keep = keep_ref[0:1]
    for row in range(1, height - 1):
        taken = window_ref[pl.ds((row - 1) * both, 3 * both), :]
        hidden_ref[pl.ds((row - 1) * channels, channels), :] = hidden_row(taken, first_w_ref, keep)
    near_ref[:both] = hidden_ref[:both]
    near_ref[both:] = hidden_ref[(height - 4) * channels :]
    part_ref[...] = jnp.zeros_like(part_ref)
    inner = range(2, height - 2)
    for index in range(len(inner)):
        taken = hidden_ref[pl.ds(index * channels, 3 * channels), :]
        second_ref[:, index * lanes : (index + 1) * lanes] = second_row(taken, second_w_ref)
    project(second_ref, inner, head_ref, part_ref)

    cells = tissue_ref[...].astype(jnp.float32)
    count = cells.shape[1]
    spread = lax.broadcasted_iota(jnp.int32, (count, lanes), 1) // BLK == lax.broadcasted_iota(jnp.int32, (count, lanes), 0)
    spread = jnp.dot(cells, spread.astype(jnp.float32), preferred_element_type=jnp.float32)
    for cell in range(cells.shape[0]):
        cover_ref[pl.ds(cell * BLK, BLK), :] = jnp.broadcast_to(spread[cell : cell + 1], (BLK, lanes))
    base_ref[...] = offsets_ref[...].astype(jnp.float32) + fractions_ref[...].astype(jnp.float32) / frac_scale
    motion_ref[...] = base_ref[...] + cover_ref[...][None] * jnp.tanh(part_ref[...])
    for row in range(2, height - 2, 2):
        first, last = max(0, row - HALO), min(height, row + HALO + 2)
        source = band_ref[pl.ds(first * channels, (last - first) * channels), :]
        hat = column_weights(motion_ref, row)
        hats_ref[row // 2 - 1] = hat
        sums_ref[pl.ds((row // 2 - 1) * channels, channels), :] = warp_part(
            motion_ref, row, hat, source, first, last - first, None
        )


def new_motion(side_ref, hidden_ref, second_ref, rows, keeps, spots, weights, field_refs, half, inner_motion_ref, residual_ref):
    first_w_ref, second_w_ref, head_ref = weights
    base_ref, cover_ref = field_refs
    both = side_ref.shape[0] // 4
    channels = both // 2
    for index, (keep, spot) in enumerate(zip(keeps, spots)):
        taken = side_ref[pl.ds(index * both, 3 * both), :]
        hidden_ref[pl.ds(spot * channels, channels), :] = hidden_row(taken, first_w_ref, keep)
    for index in range(2):
        taken = hidden_ref[pl.ds(index * channels, 3 * channels), :]
        second_ref[:, index * LANES : (index + 1) * LANES] = second_row(taken, second_w_ref)
    residual_ref[...] = jnp.zeros_like(residual_ref)
    project(second_ref, rows, head_ref, residual_ref)
    count = residual_ref.shape[1]
    block = pl.ds(half * count, count)
    fresh = base_ref[:, block, :] + cover_ref[block, :][None] * jnp.tanh(residual_ref[...])
    place = lax.broadcasted_iota(jnp.int32, fresh.shape, 1)
    is_fresh = (place == rows[0]) | (place == rows[1])
    return jnp.where(is_fresh, fresh, inner_motion_ref[:, block, :])


def top_kernel(
    keep_ref, band_ref, near_side_ref, near_ref, base_ref, cover_ref, first_w_ref, second_w_ref, sums_ref,
    inner_motion_ref, hats_ref, above_ref, head_ref,
    top_ref, motion_ref, halo_ref, side_ref, hidden_ref, second_ref, residual_ref,
):
    channels = above_ref.shape[1]
    both = 2 * channels
    middle, last = above_ref[HALO + 2].astype(jnp.float32), above_ref[HALO + 3].astype(jnp.float32)
    for index in range(HALO):
        targets = [(halo_ref, index * channels)]
        if index >= HALO - 2:
            targets.append((side_ref, (index - HALO + 2) * both))
        lay_both(above_ref[index], *((middle, index) if index < 2 else (last, index - 2)), *targets)
    for index in range(2):
        lay_both(above_ref[HALO + index], middle, 4 + index, (side_ref, index * both + channels))
    side_ref[2 * both :] = near_side_ref[: 2 * both]
    hidden_ref[both:] = near_ref[:both]
    keeps = (keep_ref[1:2], keep_ref[0:1])
    weights = (first_w_ref, second_w_ref, head_ref)
    motion_ref[...] = new_motion(
        side_ref, hidden_ref, second_ref, (0, 1), keeps, (0, 1), weights, (base_ref, cover_ref), 0, inner_motion_ref, residual_ref
    )
    for row in (2, 4, 6, 8):
        total = sums_ref[pl.ds((row // 2 - 1) * channels, channels), :]
        source = halo_ref[row * channels :, :]
        total = warp_part(inner_motion_ref, row, hats_ref[row // 2 - 1], source, row - HALO, HALO - row, total)
        top_ref[pl.ds(row // 2 * channels, channels), :] = total
    hat = column_weights(motion_ref, 0)
    total = warp_part(motion_ref, 0, hat, halo_ref[...], -HALO, HALO, None)
    top_ref[:channels, :] = warp_part(motion_ref, 0, hat, band_ref[: (HALO + 2) * channels, :], 0, HALO + 2, total)


def bottom_kernel(
    keep_ref, band_ref, near_side_ref, near_ref, base_ref, cover_ref, first_w_ref, second_w_ref, sums_ref,
    inner_motion_ref, hats_ref, top_ref, top_motion_ref, below_ref, head_ref,
    warped_ref, field_ref, halo_ref, side_ref, hidden_ref, second_ref, residual_ref, motion_ref, rows_ref, staged_ref, sems,
):
    channels, height, lanes = warped_ref.shape
    both = 2 * channels
    half = height // 2
    first, center = below_ref[HALO + 2].astype(jnp.float32), below_ref[HALO + 3].astype(jnp.float32)
    for index in range(HALO):
        targets = [(halo_ref, index * channels)]
        if index < 2:
            targets.append((side_ref, (2 + index) * both))
        lay_both(below_ref[index], *((first, index) if index < 7 else (center, index - 7)), *targets)
    for index in range(2):
        lay_both(below_ref[HALO + index], center, 2 + index, (side_ref, (2 + index) * both + channels))
    side_ref[: 2 * both] = near_side_ref[2 * both :]
    hidden_ref[:both] = near_ref[both:]
    keeps = (keep_ref[0:1], keep_ref[2:3])
    weights = (first_w_ref, second_w_ref, head_ref)
    motion_ref[:, :half, :] = top_motion_ref[...]
    motion_ref[:, half:, :] = new_motion(
        side_ref, hidden_ref, second_ref, (half - 2, half - 1), keeps, (2, 3), weights, (base_ref, cover_ref), 1,
        inner_motion_ref, residual_ref,
    )
    field_copy = pltpu.make_async_copy(motion_ref, field_ref, sems.at[4])
    field_copy.start()

    def keep_rows(row, total):
        rows_ref[pl.ds(row * channels, channels), :] = total[:, :lanes]
        rows_ref[pl.ds((row + 1) * channels, channels), :] = total[:, lanes:]

    for row in (0, 2, 4):
        keep_rows(row, top_ref[pl.ds(row // 2 * channels, channels), :])
    for row in (6, 8, 10, 12):
        if row < HALO:
            total = top_ref[pl.ds(row // 2 * channels, channels), :]
        else:
            total = sums_ref[pl.ds((row // 2 - 1) * channels, channels), :]
        count = row + HALO + 2 - height
        source = halo_ref[: count * channels, :]
        keep_rows(row, warp_part(inner_motion_ref, row, hats_ref[row // 2 - 1], source, height, count, total))
        if row == 6:
            for ch in range(channels):
                value = rows_ref[pl.ds(ch, half, stride=channels), :]
                staged_ref[ch, :half, :] = value.astype(jnp.bfloat16)
    row = height - 2
    start = row - HALO
    hat = column_weights(motion_ref, row)
    total = warp_part(motion_ref, row, hat, band_ref[start * channels :, :], start, HALO + 2, None)
    keep_rows(row, warp_part(motion_ref, row, hat, halo_ref[...], height, HALO, total))
    copies = []
    piece = channels // 4
    for part in range(4):
        for ch in range(part * piece, (part + 1) * piece):
            value = rows_ref[pl.ds(half * channels + ch, half, stride=channels), :]
            staged_ref[ch, half:, :] = value.astype(jnp.bfloat16)
        block = pl.ds(part * piece, piece)
        copies.append(pltpu.make_async_copy(staged_ref.at[block], warped_ref.at[block], sems.at[part]))
        copies[-1].start()
    for copy in (field_copy, *copies):
        copy.wait()


VMEM = pl.BlockSpec(memory_space=pltpu.VMEM)


def call(body, outputs, scratch, *operands, flops=0, placed=()):
    moved = sum(x.size * x.dtype.itemsize for x in (*operands, *outputs))
    return pl.pallas_call(
        body,
        out_shape=outputs,
        in_specs=[VMEM] * len(operands),
        out_specs=[pl.BlockSpec(memory_space=pl.ANY) if i in placed else VMEM for i in range(len(outputs))],
        scratch_shapes=scratch,
        compiler_params=pltpu.CompilerParams(vmem_limit_bytes=40 * 2**20),
        cost_estimate=pl.CostEstimate(flops=flops, bytes_accessed=moved, transcendentals=0),
    )(*operands)


def of(shape, dtype=jnp.bfloat16):
    return jax.ShapeDtypeStruct(shape, dtype)


def ring(value, axis, step):
    peers = lax.axis_size(axis)
    return lax.ppermute(value, axis, [(i, (i + step) % peers) for i in range(peers)])


def across(value, step):
    rows, cols = lax.axis_size("row"), lax.axis_size("col")
    place = lambda pair, row, col: (pair * rows + row) * cols + col
    pairs = [
        (place(pair, row, col), place(1 - pair, row + step, col))
        for pair in range(2)
        for row in range(rows)
        if 0 <= row + step < rows
        for col in range(cols)
    ]
    return lax.ppermute(value, ("pair", "row", "col"), pairs)


def shards(features, offsets, fractions, tissue, w_first, w_second, head_weight):
    _, channels, height, columns = features.shape
    f32, bf16 = jnp.float32, jnp.bfloat16
    row, col = lax.axis_index("row"), lax.axis_index("col")
    rows, cols = lax.axis_size("row"), lax.axis_size("col")
    ring_lane = jnp.arange(RING)[None]
    inside = ((col > 0) | (ring_lane != RING - 1)) & ((col < cols - 1) | (ring_lane != LANES))
    line = jnp.arange(8)[:, None]
    keep = (inside & ((line != 1) | (row > 0)) & ((line != 2) | (row < rows - 1))).astype(f32)

    swap = [(0, 1), (1, 0)]
    partner = lax.ppermute(features[0], "pair", swap)
    tile_shape = (height, channels, columns)
    scratch = [pltpu.VMEM((height * channels, columns), f32)]
    own_tile, edge = call(pack_kernel, [of(tile_shape), of((3, channels, columns))], scratch, features[0])
    from_left = ring(edge, "col", 1)
    from_right = ring(edge, "col", -1)
    lane = jnp.arange(columns)
    joined = jnp.where(
        lane % PITCH < HALO,
        jnp.where(col == 0, jnp.zeros_like(from_left), from_left),
        jnp.where(col == cols - 1, jnp.zeros_like(from_right), from_right),
    )
    both_joined = lax.all_gather(joined, "pair")
    other_joined = jnp.where(lax.axis_index("pair") == 0, both_joined[1], both_joined[0])
    (other_tile,) = call(transpose_kernel, [of(tile_shape)], scratch, partner)
    mixed = jnp.where(lane < 2 * PITCH, other_joined[1], joined[1])[None]
    above = across(jnp.concatenate([other_tile[height - HALO :], own_tile[height - 2 :], mixed, other_joined[2:]]), 1)
    below = across(jnp.concatenate([other_tile[:HALO], own_tile[:2], other_joined[:1], mixed]), -1)

    wide = height * channels
    band, side, near, base, cover, first_w, second_w, sums, inner_motion, hats = call(
        middle_kernel,
        [
            of((wide, RING)),
            of((8 * channels, RING)),
            of((4 * channels, RING)),
            of((2, height, columns), f32),
            of((height, columns), f32),
            of((3 * channels, 6 * channels)),
            of((3 * channels, 3 * channels)),
            of(((height // 2 - 2) * channels, RING), f32),
            of((2, height, columns), f32),
            of((height // 2 - 2, RING, RING)),
        ],
        [
            pltpu.VMEM((2 * wide, RING), bf16),
            pltpu.VMEM(((height - 2) * channels, RING), bf16),
            pltpu.VMEM((channels, (height - 4) * columns), bf16),
            pltpu.VMEM((2, height, columns), f32),
        ],
        keep, own_tile, other_tile, joined, other_joined,
        w_first, w_second, head_weight, offsets[0], fractions[0], tissue[0],
        flops=4 * 10**9,
    )
    common = (keep, band, side, near, base, cover, first_w, second_w, sums, inner_motion, hats)
    edge_scratch = [
        pltpu.VMEM((HALO * channels, RING), bf16),
        pltpu.VMEM((8 * channels, RING), bf16),
        pltpu.VMEM((4 * channels, RING), bf16),
        pltpu.VMEM((channels, 2 * columns), bf16),
        pltpu.VMEM((2, height // 2, columns), f32),
    ]
    top, top_motion = call(
        top_kernel,
        [of((5 * channels, RING), f32), of((2, height // 2, columns), f32)],
        edge_scratch,
        *common, above, head_weight,
        flops=10**9,
    )
    warped, motion = call(
        bottom_kernel,
        [of((channels, height, columns)), of((2, height, columns), f32)],
        [
            *edge_scratch,
            pltpu.VMEM((2, height, columns), f32),
            pltpu.VMEM((wide, columns), f32),
            pltpu.VMEM((channels, height, columns), bf16),
            pltpu.SemaphoreType.DMA((5,)),
        ],
        *common, top, top_motion, below, head_weight,
        flops=10**9, placed=(0, 1),
    )
    return (warped[None], motion[None])


def solution(mesh):
    return jax.shard_map(
        shards,
        mesh=mesh,
        in_specs=(
            P("pair", None, "row", "col"),
            P("pair", None, "row", "col"),
            P("pair", None, "row", "col"),
            P("pair", "row", "col"),
            P(),
            P(),
            P(),
        ),
        out_specs=(P("pair", None, "row", "col"), P("pair", None, "row", "col")),
        check_vma=False,
    )
```

```python
import functools

import jax
import jax.numpy as jnp
from jax import lax
from jax.experimental import pallas as pl
from jax.experimental.pallas import tpu as pltpu
from jax.sharding import PartitionSpec as P

MAXS = 8
BLK = 8
CH = 64
HALO = MAXS + 1
LANES = 128
RING = 2 * LANES
PITCH = 2 * HALO
GROUPS = ((0, 7), (7, 9), (9, 16))


def EXTRA(height):
    return [0, 1, height - 2, height - 1]


frac_scale = 256.0


def lane_iota(shape):
    return lax.broadcasted_iota(jnp.int32, shape, len(shape) - 1)


def packed_edge(value, slot):
    return pltpu.roll(value, (PITCH * slot + HALO) % LANES, 1)


def in_slot(lane, slot):
    return (lane >= PITCH * slot) & (lane < PITCH * (slot + 1))


def border_of(vector, slot):
    return pltpu.roll(vector, (-PITCH * slot - HALO) % LANES, 1)


def pack_kernel(feat_ref, tile_ref, edge_ref, rows_ref):
    channels, height, lanes = feat_ref.shape
    for ch in range(channels):
        rows_ref[pl.ds(ch * height, height), :] = feat_ref[ch].astype(jnp.float32)
    lane = lane_iota((channels, lanes))
    for group, (first, last) in enumerate(GROUPS):
        packed = jnp.zeros((channels, lanes), jnp.float32)
        taken = list(range(first, last))
        if group == 1:
            taken += EXTRA(height)
        for slot, row in enumerate(taken):
            value = rows_ref[pl.ds(row, channels, stride=height), :]
            if slot < last - first:
                tile_ref[row] = value.astype(jnp.bfloat16)
            packed = jnp.where(in_slot(lane, slot), packed_edge(value, slot), packed)
        edge_ref[group] = packed.astype(jnp.bfloat16)


def shifted_sum(stacked):
    count = stacked.shape[0] // 3
    left = pltpu.roll(stacked[:count], 1, 1)
    right = pltpu.roll(stacked[2 * count :], RING - 1, 1)
    return left + stacked[count : 2 * count] + right


def hidden_row(taken, first_w_ref, keep):
    total = jnp.dot(first_w_ref[...], taken, preferred_element_type=jnp.float32)
    return (jnp.maximum(shifted_sum(total), 0.0) * keep).astype(jnp.bfloat16)


def second_row(taken, second_w_ref):
    total = jnp.dot(second_w_ref[...], taken, preferred_element_type=jnp.float32)
    return jnp.maximum(shifted_sum(total)[:, :LANES], 0.0).astype(jnp.bfloat16)


def project(second_ref, rows, head_ref, residual_ref):
    pairs = jnp.dot(head_ref[...], second_ref[...], preferred_element_type=jnp.float32)
    for index, row in enumerate(rows):
        for k in range(2):
            residual_ref[k, pl.ds(row, 1), :] = pairs[k : k + 1, index * LANES : (index + 1) * LANES]


def two_rows(motion_ref, k, row):
    return jnp.concatenate([motion_ref[k, row : row + 1, :], motion_ref[k, row + 1 : row + 2, :]], axis=1)


def column_weights(motion_ref, row):
    place = (lane_iota((1, RING)) & (LANES - 1)).astype(jnp.float32) + two_rows(motion_ref, 1, row)
    parts = []
    for first, count in ((0, LANES + 16), (-16, 16)):
        column = (lax.broadcasted_iota(jnp.int32, (count, RING), 0) + first).astype(jnp.float32)
        parts.append(jnp.maximum(1.0 - jnp.abs(place - column), 0.0).astype(jnp.bfloat16))
    return jnp.concatenate([parts[0], jnp.zeros((RING - LANES - 32, RING), jnp.bfloat16), parts[1]])


def warp_part(motion_ref, row, hat, source, first, count, total):
    mixed = jnp.dot(source, hat, preferred_element_type=jnp.float32)
    place = jnp.where(lane_iota((1, RING)) < LANES, 0.0, 1.0) + two_rows(motion_ref, 0, row)
    channels = source.shape[0] // count
    for step in range(count):
        weight = jnp.maximum(1.0 - jnp.abs(place - (first + step - row)), 0.0)
        term = weight * mixed[step * channels : (step + 1) * channels]
        total = term if total is None else total + term
    return total


def lay_both(tile, vector, slot, *targets):
    border = border_of(vector, slot).astype(jnp.bfloat16)
    for ref, start in targets:
        block = pl.ds(start, tile.shape[0])
        ref[block, :LANES] = tile
        ref[block, LANES:] = border


def middle_kernel(
    keep_ref, own_tile_ref, other_tile_ref, own_joined_ref, other_joined_ref,
    w_first_ref, w_second_ref, head_ref, offsets_ref, fractions_ref, tissue_ref,
    band_ref, side_ref, near_ref, base_ref, cover_ref, first_w_ref, second_w_ref, sums_ref, motion_ref, hats_ref,
    window_ref, hidden_ref, second_ref, part_ref,
):
    height, channels, lanes = own_tile_ref.shape
    both = 2 * channels
    for b in range(3):
        block = pl.ds(b * channels, channels)
        for a in range(3):
            first_w_ref[block, a * both : (a + 1) * both] = w_first_ref[3 * a + b]
        second_w_ref[block, :both] = jnp.concatenate([w_second_ref[b], w_second_ref[3 + b]], axis=1)
        second_w_ref[block, both:] = w_second_ref[6 + b]
    for group, (first, last) in enumerate(GROUPS):
        own_vector = own_joined_ref[group].astype(jnp.float32)
        other_vector = other_joined_ref[group].astype(jnp.float32)
        for row in range(first, last):
            lay_both(own_tile_ref[row], own_vector, row - first, (band_ref, row * channels), (window_ref, row * both))
            lay_both(other_tile_ref[row], other_vector, row - first, (window_ref, row * both + channels))
    side_ref[: 2 * both] = window_ref[: 2 * both]
    side_ref[2 * both :] = window_ref[(height - 2) * both :]
    keep = keep_ref[0:1]
    for row in range(1, height - 1):
        taken = window_ref[pl.ds((row - 1) * both, 3 * both), :]
        hidden_ref[pl.ds((row - 1) * channels, channels), :] = hidden_row(taken, first_w_ref, keep)
    near_ref[:both] = hidden_ref[:both]
    near_ref[both:] = hidden_ref[(height - 4) * channels :]
    part_ref[...] = jnp.zeros_like(part_ref)
    inner = range(2, height - 2)
    for index in range(len(inner)):
        taken = hidden_ref[pl.ds(index * channels, 3 * channels), :]
        second_ref[:, index * lanes : (index + 1) * lanes] = second_row(taken, second_w_ref)
    project(second_ref, inner, head_ref, part_ref)

    cells = tissue_ref[...].astype(jnp.float32)
    count = cells.shape[1]
    spread = lax.broadcasted_iota(jnp.int32, (count, lanes), 1) // BLK == lax.broadcasted_iota(jnp.int32, (count, lanes), 0)
    spread = jnp.dot(cells, spread.astype(jnp.float32), preferred_element_type=jnp.float32)
    for cell in range(cells.shape[0]):
        cover_ref[pl.ds(cell * BLK, BLK), :] = jnp.broadcast_to(spread[cell : cell + 1], (BLK, lanes))
    base_ref[...] = offsets_ref[...].astype(jnp.float32) + fractions_ref[...].astype(jnp.float32) / frac_scale
    motion_ref[...] = base_ref[...] + cover_ref[...][None] * jnp.tanh(part_ref[...])
    for row in range(2, height - 2, 2):
        first, last = max(0, row - HALO), min(height, row + HALO + 2)
        source = band_ref[pl.ds(first * channels, (last - first) * channels), :]
        hat = column_weights(motion_ref, row)
        hats_ref[row // 2 - 1] = hat
        sums_ref[pl.ds((row // 2 - 1) * channels, channels), :] = warp_part(
            motion_ref, row, hat, source, first, last - first, None
        )


def new_motion(side_ref, hidden_ref, second_ref, rows, keeps, spots, weights, field_refs, half, inner_motion_ref, residual_ref):
    first_w_ref, second_w_ref, head_ref = weights
    base_ref, cover_ref = field_refs
    both = side_ref.shape[0] // 4
    channels = both // 2
    for index, (keep, spot) in enumerate(zip(keeps, spots)):
        taken = side_ref[pl.ds(index * both, 3 * both), :]
        hidden_ref[pl.ds(spot * channels, channels), :] = hidden_row(taken, first_w_ref, keep)
    for index in range(2):
        taken = hidden_ref[pl.ds(index * channels, 3 * channels), :]
        second_ref[:, index * LANES : (index + 1) * LANES] = second_row(taken, second_w_ref)
    residual_ref[...] = jnp.zeros_like(residual_ref)
    project(second_ref, rows, head_ref, residual_ref)
    count = residual_ref.shape[1]
    block = pl.ds(half * count, count)
    fresh = base_ref[:, block, :] + cover_ref[block, :][None] * jnp.tanh(residual_ref[...])
    place = lax.broadcasted_iota(jnp.int32, fresh.shape, 1)
    is_fresh = (place == rows[0]) | (place == rows[1])
    return jnp.where(is_fresh, fresh, inner_motion_ref[:, block, :])


def top_kernel(
    keep_ref, band_ref, near_side_ref, near_ref, base_ref, cover_ref, first_w_ref, second_w_ref, sums_ref,
    inner_motion_ref, hats_ref, above_ref, head_ref,
    top_ref, motion_ref, halo_ref, side_ref, hidden_ref, second_ref, residual_ref,
):
    channels = above_ref.shape[1]
    both = 2 * channels
    middle, last = above_ref[HALO + 2].astype(jnp.float32), above_ref[HALO + 3].astype(jnp.float32)
    for index in range(HALO):
        targets = [(halo_ref, index * channels)]
        if index >= HALO - 2:
            targets.append((side_ref, (index - HALO + 2) * both))
        lay_both(above_ref[index], *((middle, index) if index < 2 else (last, index - 2)), *targets)
    for index in range(2):
        lay_both(above_ref[HALO + index], middle, 4 + index, (side_ref, index * both + channels))
    side_ref[2 * both :] = near_side_ref[: 2 * both]
    hidden_ref[both:] = near_ref[:both]
    keeps = (keep_ref[1:2], keep_ref[0:1])
    weights = (first_w_ref, second_w_ref, head_ref)
    motion_ref[...] = new_motion(
        side_ref, hidden_ref, second_ref, (0, 1), keeps, (0, 1), weights, (base_ref, cover_ref), 0, inner_motion_ref, residual_ref
    )
    for row in (2, 4, 6, 8):
        total = sums_ref[pl.ds((row // 2 - 1) * channels, channels), :]
        source = halo_ref[row * channels :, :]
        total = warp_part(inner_motion_ref, row, hats_ref[row // 2 - 1], source, row - HALO, HALO - row, total)
        top_ref[pl.ds(row // 2 * channels, channels), :] = total
    hat = column_weights(motion_ref, 0)
    total = warp_part(motion_ref, 0, hat, halo_ref[...], -HALO, HALO, None)
    top_ref[:channels, :] = warp_part(motion_ref, 0, hat, band_ref[: (HALO + 2) * channels, :], 0, HALO + 2, total)


def bottom_kernel(
    keep_ref, band_ref, near_side_ref, near_ref, base_ref, cover_ref, first_w_ref, second_w_ref, sums_ref,
    inner_motion_ref, hats_ref, top_ref, top_motion_ref, below_ref, head_ref,
    warped_ref, field_ref, halo_ref, side_ref, hidden_ref, second_ref, residual_ref, motion_ref, rows_ref, staged_ref, sems,
):
    channels, height, lanes = warped_ref.shape
    both = 2 * channels
    half = height // 2
    first, center = below_ref[HALO + 2].astype(jnp.float32), below_ref[HALO + 3].astype(jnp.float32)
    for index in range(HALO):
        targets = [(halo_ref, index * channels)]
        if index < 2:
            targets.append((side_ref, (2 + index) * both))
        lay_both(below_ref[index], *((first, index) if index < 7 else (center, index - 7)), *targets)
    for index in range(2):
        lay_both(below_ref[HALO + index], center, 2 + index, (side_ref, (2 + index) * both + channels))
    side_ref[: 2 * both] = near_side_ref[2 * both :]
    hidden_ref[:both] = near_ref[both:]
    keeps = (keep_ref[0:1], keep_ref[2:3])
    weights = (first_w_ref, second_w_ref, head_ref)
    motion_ref[:, :half, :] = top_motion_ref[...]
    motion_ref[:, half:, :] = new_motion(
        side_ref, hidden_ref, second_ref, (half - 2, half - 1), keeps, (2, 3), weights, (base_ref, cover_ref), 1,
        inner_motion_ref, residual_ref,
    )
    field_copy = pltpu.make_async_copy(motion_ref, field_ref, sems.at[4])
    field_copy.start()

    def keep_rows(row, total):
        rows_ref[pl.ds(row * channels, channels), :] = total[:, :lanes]
        rows_ref[pl.ds((row + 1) * channels, channels), :] = total[:, lanes:]

    for row in (0, 2, 4):
        keep_rows(row, top_ref[pl.ds(row // 2 * channels, channels), :])
    for row in (6, 8, 10, 12):
        if row < HALO:
            total = top_ref[pl.ds(row // 2 * channels, channels), :]
        else:
            total = sums_ref[pl.ds((row // 2 - 1) * channels, channels), :]
        count = row + HALO + 2 - height
        source = halo_ref[: count * channels, :]
        keep_rows(row, warp_part(inner_motion_ref, row, hats_ref[row // 2 - 1], source, height, count, total))
        if row == 6:
            for ch in range(channels):
                value = rows_ref[pl.ds(ch, half, stride=channels), :]
                staged_ref[ch, :half, :] = value.astype(jnp.bfloat16)
    row = height - 2
    start = row - HALO
    hat = column_weights(motion_ref, row)
    total = warp_part(motion_ref, row, hat, band_ref[start * channels :, :], start, HALO + 2, None)
    keep_rows(row, warp_part(motion_ref, row, hat, halo_ref[...], height, HALO, total))
    copies = []
    piece = channels // 4
    for part in range(4):
        for ch in range(part * piece, (part + 1) * piece):
            value = rows_ref[pl.ds(half * channels + ch, half, stride=channels), :]
            staged_ref[ch, half:, :] = value.astype(jnp.bfloat16)
        block = pl.ds(part * piece, piece)
        copies.append(pltpu.make_async_copy(staged_ref.at[block], warped_ref.at[block], sems.at[part]))
        copies[-1].start()
    for copy in (field_copy, *copies):
        copy.wait()


VMEM = pl.BlockSpec(memory_space=pltpu.VMEM)


def call(body, outputs, scratch, *operands, flops=0, placed=()):
    moved = sum(x.size * x.dtype.itemsize for x in (*operands, *outputs))
    return pl.pallas_call(
        body,
        out_shape=outputs,
        in_specs=[VMEM] * len(operands),
        out_specs=[pl.BlockSpec(memory_space=pl.ANY) if i in placed else VMEM for i in range(len(outputs))],
        scratch_shapes=scratch,
        compiler_params=pltpu.CompilerParams(vmem_limit_bytes=40 * 2**20),
        cost_estimate=pl.CostEstimate(flops=flops, bytes_accessed=moved, transcendentals=0),
    )(*operands)


def of(shape, dtype=jnp.bfloat16):
    return jax.ShapeDtypeStruct(shape, dtype)


def ring(value, axis, step):
    peers = lax.axis_size(axis)
    return lax.ppermute(value, axis, [(i, (i + step) % peers) for i in range(peers)])


def across(value, step):
    rows, cols = lax.axis_size("row"), lax.axis_size("col")
    place = lambda pair, row, col: (pair * rows + row) * cols + col
    pairs = [
        (place(pair, row, col), place(1 - pair, row + step, col))
        for pair in range(2)
        for row in range(rows)
        if 0 <= row + step < rows
        for col in range(cols)
    ]
    return lax.ppermute(value, ("pair", "row", "col"), pairs)


def shards(features, offsets, fractions, tissue, w_first, w_second, head_weight):
    _, channels, height, columns = features.shape
    f32, bf16 = jnp.float32, jnp.bfloat16
    row, col = lax.axis_index("row"), lax.axis_index("col")
    rows, cols = lax.axis_size("row"), lax.axis_size("col")
    ring_lane = jnp.arange(RING)[None]
    inside = ((col > 0) | (ring_lane != RING - 1)) & ((col < cols - 1) | (ring_lane != LANES))
    line = jnp.arange(8)[:, None]
    keep = (inside & ((line != 1) | (row > 0)) & ((line != 2) | (row < rows - 1))).astype(f32)

    swap = [(0, 1), (1, 0)]
    tile_shape = (height, channels, columns)
    scratch = [pltpu.VMEM((height * channels, columns), f32)]
    own_tile, edge = call(pack_kernel, [of(tile_shape), of((3, channels, columns))], scratch, features[0])
    from_left = ring(edge, "col", 1)
    from_right = ring(edge, "col", -1)
    other_tile = lax.ppermute(own_tile, "pair", swap)
    lane = jnp.arange(columns)
    joined = jnp.where(
        lane % PITCH < HALO,
        jnp.where(col == 0, jnp.zeros_like(from_left), from_left),
        jnp.where(col == cols - 1, jnp.zeros_like(from_right), from_right),
    )
    both_joined = lax.all_gather(joined, "pair")
    other_joined = jnp.where(lax.axis_index("pair") == 0, both_joined[1], both_joined[0])
    mixed = jnp.where(lane < 2 * PITCH, other_joined[1], joined[1])[None]
    above = across(jnp.concatenate([other_tile[height - HALO :], own_tile[height - 2 :], mixed, other_joined[2:]]), 1)
    below = across(jnp.concatenate([other_tile[:HALO], own_tile[:2], other_joined[:1], mixed]), -1)

    wide = height * channels
    band, side, near, base, cover, first_w, second_w, sums, inner_motion, hats = call(
        middle_kernel,
        [
            of((wide, RING)),
            of((8 * channels, RING)),
            of((4 * channels, RING)),
            of((2, height, columns), f32),
            of((height, columns), f32),
            of((3 * channels, 6 * channels)),
            of((3 * channels, 3 * channels)),
            of(((height // 2 - 2) * channels, RING), f32),
            of((2, height, columns), f32),
            of((height // 2 - 2, RING, RING)),
        ],
        [
            pltpu.VMEM((2 * wide, RING), bf16),
            pltpu.VMEM(((height - 2) * channels, RING), bf16),
            pltpu.VMEM((channels, (height - 4) * columns), bf16),
            pltpu.VMEM((2, height, columns), f32),
        ],
        keep, own_tile, other_tile, joined, other_joined,
        w_first, w_second, head_weight, offsets[0], fractions[0], tissue[0],
        flops=4 * 10**9,
    )
    common = (keep, band, side, near, base, cover, first_w, second_w, sums, inner_motion, hats)
    edge_scratch = [
        pltpu.VMEM((HALO * channels, RING), bf16),
        pltpu.VMEM((8 * channels, RING), bf16),
        pltpu.VMEM((4 * channels, RING), bf16),
        pltpu.VMEM((channels, 2 * columns), bf16),
        pltpu.VMEM((2, height // 2, columns), f32),
    ]
    top, top_motion = call(
        top_kernel,
        [of((5 * channels, RING), f32), of((2, height // 2, columns), f32)],
        edge_scratch,
        *common, above, head_weight,
        flops=10**9,
    )
    warped, motion = call(
        bottom_kernel,
        [of((channels, height, columns)), of((2, height, columns), f32)],
        [
            *edge_scratch,
            pltpu.VMEM((2, height, columns), f32),
            pltpu.VMEM((wide, columns), f32),
            pltpu.VMEM((channels, height, columns), bf16),
            pltpu.SemaphoreType.DMA((5,)),
        ],
        *common, top, top_motion, below, head_weight,
        flops=10**9, placed=(0, 1),
    )
    return (warped[None], motion[None])


def solution(mesh):
    return jax.shard_map(
        shards,
        mesh=mesh,
        in_specs=(
            P("pair", None, "row", "col"),
            P("pair", None, "row", "col"),
            P("pair", None, "row", "col"),
            P("pair", "row", "col"),
            P(),
            P(),
            P(),
        ),
        out_specs=(P("pair", None, "row", "col"), P("pair", None, "row", "col")),
        check_vma=False,
    )
```

```python
import functools

import jax
import jax.numpy as jnp
from jax import lax
from jax.experimental import pallas as pl
from jax.experimental.pallas import tpu as pltpu
from jax.sharding import PartitionSpec as P

MAXS = 8
BLK = 8
CH = 64
HALO = MAXS + 1
LANES = 128
REACH = 2
RING = 2 * LANES
PITCH = 2 * HALO
GROUPS = ((0, 7), (7, 9), (9, 16))


frac_scale = 256.0


def lane_iota(shape):
    return lax.broadcasted_iota(jnp.int32, shape, len(shape) - 1)


def middle_of(slot):
    return PITCH * slot + HALO


def middle_of_extra(index):
    return 2 * PITCH + 2 * REACH * index + REACH


def border_of(vector, at):
    return pltpu.roll(vector, -at % LANES, 1)


def pack_kernel(feat_ref, tile_ref, edge_ref, rows_ref):
    channels, height, lanes = feat_ref.shape
    for ch in range(channels):
        rows_ref[pl.ds(ch * height, height), :] = feat_ref[ch].astype(jnp.float32)
    lane = lane_iota((channels, lanes))
    for group, (first, last) in enumerate(GROUPS):
        packed = jnp.zeros((channels, lanes), jnp.float32)
        taken = [(row, middle_of(row - first), HALO) for row in range(first, last)]
        if group == 1:
            taken += [(row, middle_of_extra(i), REACH) for i, row in enumerate((0, 1, height - 2, height - 1))]
        for row, at, wide in taken:
            value = rows_ref[pl.ds(row, channels, stride=height), :]
            if wide == HALO:
                tile_ref[row] = value.astype(jnp.bfloat16)
            packed = jnp.where((lane >= at - wide) & (lane < at + wide), pltpu.roll(value, at % lanes, 1), packed)
        edge_ref[group] = packed.astype(jnp.bfloat16)


def shifted_sum(stacked):
    count = stacked.shape[0] // 3
    left = pltpu.roll(stacked[:count], 1, 1)
    right = pltpu.roll(stacked[2 * count :], RING - 1, 1)
    return left + stacked[count : 2 * count] + right


def hidden_row(taken, first_w_ref, keep):
    total = jnp.dot(first_w_ref[...], taken, preferred_element_type=jnp.float32)
    return (jnp.maximum(shifted_sum(total), 0.0) * keep).astype(jnp.bfloat16)


def second_row(taken, second_w_ref):
    total = jnp.dot(second_w_ref[...], taken, preferred_element_type=jnp.float32)
    return jnp.maximum(shifted_sum(total)[:, :LANES], 0.0).astype(jnp.bfloat16)


def project(second_ref, rows, head_ref, residual_ref):
    pairs = jnp.dot(head_ref[...], second_ref[...], preferred_element_type=jnp.float32)
    for index, row in enumerate(rows):
        for k in range(2):
            residual_ref[k, pl.ds(row, 1), :] = pairs[k : k + 1, index * LANES : (index + 1) * LANES]


def two_rows(motion_ref, k, row):
    return jnp.concatenate([motion_ref[k, row : row + 1, :], motion_ref[k, row + 1 : row + 2, :]], axis=1)


def column_weights(motion_ref, row):
    place = (lane_iota((1, RING)) & (LANES - 1)).astype(jnp.float32) + two_rows(motion_ref, 1, row)
    parts = []
    for first, count in ((0, LANES + 16), (-16, 16)):
        column = (lax.broadcasted_iota(jnp.int32, (count, RING), 0) + first).astype(jnp.float32)
        parts.append(jnp.maximum(1.0 - jnp.abs(place - column), 0.0).astype(jnp.bfloat16))
    return jnp.concatenate([parts[0], jnp.zeros((RING - LANES - 32, RING), jnp.bfloat16), parts[1]])


def warp_part(motion_ref, row, hat, source, first, count, total):
    mixed = jnp.dot(source, hat, preferred_element_type=jnp.float32)
    place = jnp.where(lane_iota((1, RING)) < LANES, 0.0, 1.0) + two_rows(motion_ref, 0, row)
    channels = source.shape[0] // count
    for step in range(count):
        weight = jnp.maximum(1.0 - jnp.abs(place - (first + step - row)), 0.0)
        term = weight * mixed[step * channels : (step + 1) * channels]
        total = term if total is None else total + term
    return total


def lay_both(tile, vector, at, *targets):
    border = border_of(vector, at).astype(jnp.bfloat16)
    for ref, start in targets:
        block = pl.ds(start, tile.shape[0])
        ref[block, :LANES] = tile
        ref[block, LANES:] = border


def middle_kernel(
    keep_ref, own_tile_ref, other_tile_ref, own_joined_ref, other_joined_ref,
    w_first_ref, w_second_ref, offsets_ref, fractions_ref, head_in_ref, tissue_in_ref,
    band_ref, side_ref, near_ref, base_ref, cover_ref, first_w_ref, second_w_ref, sums_ref, motion_ref, hats_ref, head_ref,
    window_ref, hidden_ref, second_ref, part_ref, tissue_ref, sems,
):
    height, channels, lanes = own_tile_ref.shape
    copies = [
        pltpu.make_async_copy(head_in_ref, head_ref, sems.at[0]),
        pltpu.make_async_copy(tissue_in_ref, tissue_ref, sems.at[1]),
    ]
    for copy in copies:
        copy.start()
    both = 2 * channels
    for b in range(3):
        block = pl.ds(b * channels, channels)
        for a in range(3):
            first_w_ref[block, a * both : (a + 1) * both] = w_first_ref[3 * a + b]
        second_w_ref[block, :both] = jnp.concatenate([w_second_ref[b], w_second_ref[3 + b]], axis=1)
        second_w_ref[block, both:] = w_second_ref[6 + b]
    for group, (first, last) in enumerate(GROUPS):
        own_vector = own_joined_ref[group].astype(jnp.float32)
        other_vector = other_joined_ref[group].astype(jnp.float32)
        for row in range(first, last):
            lay_both(own_tile_ref[row], own_vector, middle_of(row - first), (band_ref, row * channels), (window_ref, row * both))
            lay_both(other_tile_ref[row], other_vector, middle_of(row - first), (window_ref, row * both + channels))
    side_ref[: 2 * both] = window_ref[: 2 * both]
    side_ref[2 * both :] = window_ref[(height - 2) * both :]
    keep = keep_ref[0:1]
    for row in range(1, height - 1):
        taken = window_ref[pl.ds((row - 1) * both, 3 * both), :]
        hidden_ref[pl.ds((row - 1) * channels, channels), :] = hidden_row(taken, first_w_ref, keep)
    near_ref[:both] = hidden_ref[:both]
    near_ref[both:] = hidden_ref[(height - 4) * channels :]
    part_ref[...] = jnp.zeros_like(part_ref)
    inner = range(2, height - 2)
    for index in range(len(inner)):
        taken = hidden_ref[pl.ds(index * channels, 3 * channels), :]
        second_ref[:, index * lanes : (index + 1) * lanes] = second_row(taken, second_w_ref)
    for copy in copies:
        copy.wait()
    project(second_ref, inner, head_ref, part_ref)

    cells = tissue_ref[...].astype(jnp.float32)
    count = cells.shape[1]
    spread = lax.broadcasted_iota(jnp.int32, (count, lanes), 1) // BLK == lax.broadcasted_iota(jnp.int32, (count, lanes), 0)
    spread = jnp.dot(cells, spread.astype(jnp.float32), preferred_element_type=jnp.float32)
    for cell in range(cells.shape[0]):
        cover_ref[pl.ds(cell * BLK, BLK), :] = jnp.broadcast_to(spread[cell : cell + 1], (BLK, lanes))
    base_ref[...] = offsets_ref[...].astype(jnp.float32) + fractions_ref[...].astype(jnp.float32) / frac_scale
    motion_ref[...] = base_ref[...] + cover_ref[...][None] * jnp.tanh(part_ref[...])
    for row in range(2, height - 2, 2):
        first, last = max(0, row - HALO), min(height, row + HALO + 2)
        source = band_ref[pl.ds(first * channels, (last - first) * channels), :]
        hat = column_weights(motion_ref, row)
        hats_ref[row // 2 - 1] = hat
        sums_ref[pl.ds((row // 2 - 1) * channels, channels), :] = warp_part(
            motion_ref, row, hat, source, first, last - first, None
        )


def new_motion(side_ref, hidden_ref, second_ref, rows, keeps, spots, weights, field_refs, half, inner_motion_ref, residual_ref):
    first_w_ref, second_w_ref, head_ref = weights
    base_ref, cover_ref = field_refs
    both = side_ref.shape[0] // 4
    channels = both // 2
    for index, (keep, spot) in enumerate(zip(keeps, spots)):
        taken = side_ref[pl.ds(index * both, 3 * both), :]
        hidden_ref[pl.ds(spot * channels, channels), :] = hidden_row(taken, first_w_ref, keep)
    for index in range(2):
        taken = hidden_ref[pl.ds(index * channels, 3 * channels), :]
        second_ref[:, index * LANES : (index + 1) * LANES] = second_row(taken, second_w_ref)
    residual_ref[...] = jnp.zeros_like(residual_ref)
    project(second_ref, rows, head_ref, residual_ref)
    count = residual_ref.shape[1]
    block = pl.ds(half * count, count)
    fresh = base_ref[:, block, :] + cover_ref[block, :][None] * jnp.tanh(residual_ref[...])
    place = lax.broadcasted_iota(jnp.int32, fresh.shape, 1)
    is_fresh = (place == rows[0]) | (place == rows[1])
    return jnp.where(is_fresh, fresh, inner_motion_ref[:, block, :])


def message_row(ref, index, channels):
    return ref[pl.ds(index * channels, channels), :]


def message_borders(ref, channels):
    last = (HALO + 3) * channels
    folded = ref[last:, :].astype(jnp.float32)
    unfolded = jnp.concatenate([folded, pltpu.roll(folded, LANES // 2, 1)])
    return message_row(ref, HALO + 2, channels).astype(jnp.float32), unfolded


def top_kernel(
    keep_ref, band_ref, near_side_ref, near_ref, base_ref, cover_ref, first_w_ref, second_w_ref, sums_ref,
    inner_motion_ref, hats_ref, above_ref, head_ref,
    top_ref, motion_ref, halo_ref, side_ref, hidden_ref, second_ref, residual_ref,
):
    channels = head_ref.shape[1]
    both = 2 * channels
    seven, two = message_borders(above_ref, channels)
    for index in range(HALO):
        targets = [(halo_ref, index * channels)]
        if index >= HALO - 2:
            targets.append((side_ref, (index - HALO + 2) * both))
        strip = (two, middle_of(index)) if index < 2 else (seven, middle_of(index - 2))
        lay_both(message_row(above_ref, index, channels), *strip, *targets)
    for index in range(2):
        tile = message_row(above_ref, HALO + index, channels)
        lay_both(tile, two, middle_of_extra(2 + index), (side_ref, index * both + channels))
    side_ref[2 * both :] = near_side_ref[: 2 * both]
    hidden_ref[both:] = near_ref[:both]
    keeps = (keep_ref[1:2], keep_ref[0:1])
    weights = (first_w_ref, second_w_ref, head_ref)
    motion_ref[...] = new_motion(
        side_ref, hidden_ref, second_ref, (0, 1), keeps, (0, 1), weights, (base_ref, cover_ref), 0, inner_motion_ref, residual_ref
    )
    for row in (2, 4, 6, 8):
        total = sums_ref[pl.ds((row // 2 - 1) * channels, channels), :]
        source = halo_ref[row * channels :, :]
        total = warp_part(inner_motion_ref, row, hats_ref[row // 2 - 1], source, row - HALO, HALO - row, total)
        top_ref[pl.ds(row // 2 * channels, channels), :] = total
    hat = column_weights(motion_ref, 0)
    total = warp_part(motion_ref, 0, hat, halo_ref[...], -HALO, HALO, None)
    top_ref[:channels, :] = warp_part(motion_ref, 0, hat, band_ref[: (HALO + 2) * channels, :], 0, HALO + 2, total)


def bottom_kernel(
    keep_ref, band_ref, near_side_ref, near_ref, base_ref, cover_ref, first_w_ref, second_w_ref, sums_ref,
    inner_motion_ref, hats_ref, top_ref, top_motion_ref, below_ref, head_ref,
    warped_ref, field_ref, halo_ref, side_ref, hidden_ref, second_ref, residual_ref, motion_ref, rows_ref, staged_ref, sems,
):
    channels, height, lanes = warped_ref.shape
    both = 2 * channels
    half = height // 2
    seven, two = message_borders(below_ref, channels)
    for index in range(HALO):
        targets = [(halo_ref, index * channels)]
        if index < 2:
            targets.append((side_ref, (2 + index) * both))
        strip = (seven, middle_of(index)) if index < 7 else (two, middle_of(index - 7))
        lay_both(message_row(below_ref, index, channels), *strip, *targets)
    for index in range(2):
        tile = message_row(below_ref, HALO + index, channels)
        lay_both(tile, two, middle_of_extra(index), (side_ref, (2 + index) * both + channels))
    side_ref[: 2 * both] = near_side_ref[2 * both :]
    hidden_ref[:both] = near_ref[both:]
    keeps = (keep_ref[0:1], keep_ref[2:3])
    weights = (first_w_ref, second_w_ref, head_ref)
    motion_ref[:, :half, :] = top_motion_ref[...]
    motion_ref[:, half:, :] = new_motion(
        side_ref, hidden_ref, second_ref, (half - 2, half - 1), keeps, (2, 3), weights, (base_ref, cover_ref), 1,
        inner_motion_ref, residual_ref,
    )
    field_copy = pltpu.make_async_copy(motion_ref, field_ref, sems.at[4])
    field_copy.start()

    def keep_rows(row, total):
        rows_ref[pl.ds(row * channels, channels), :] = total[:, :lanes]
        rows_ref[pl.ds((row + 1) * channels, channels), :] = total[:, lanes:]

    for row in (0, 2, 4):
        keep_rows(row, top_ref[pl.ds(row // 2 * channels, channels), :])
    for row in (6, 8, 10, 12):
        if row < HALO:
            total = top_ref[pl.ds(row // 2 * channels, channels), :]
        else:
            total = sums_ref[pl.ds((row // 2 - 1) * channels, channels), :]
        count = row + HALO + 2 - height
        source = halo_ref[: count * channels, :]
        keep_rows(row, warp_part(inner_motion_ref, row, hats_ref[row // 2 - 1], source, height, count, total))
        if row == 6:
            for ch in range(channels):
                value = rows_ref[pl.ds(ch, half, stride=channels), :]
                staged_ref[ch, :half, :] = value.astype(jnp.bfloat16)
            upper = pl.ds(0, half)
            upper_copy = pltpu.make_async_copy(staged_ref.at[:, upper], warped_ref.at[:, upper], sems.at[5])
            upper_copy.start()
    row = height - 2
    start = row - HALO
    hat = column_weights(motion_ref, row)
    total = warp_part(motion_ref, row, hat, band_ref[start * channels :, :], start, HALO + 2, None)
    keep_rows(row, warp_part(motion_ref, row, hat, halo_ref[...], height, HALO, total))
    copies = []
    piece = channels // 4
    for part in range(4):
        for ch in range(part * piece, (part + 1) * piece):
            value = rows_ref[pl.ds(half * channels + ch, half, stride=channels), :]
            staged_ref[ch, half:, :] = value.astype(jnp.bfloat16)
        block, lower = pl.ds(part * piece, piece), pl.ds(half, half)
        copies.append(pltpu.make_async_copy(staged_ref.at[block, lower], warped_ref.at[block, lower], sems.at[part]))
        copies[-1].start()
    for copy in (field_copy, upper_copy, *copies):
        copy.wait()


VMEM = pl.BlockSpec(memory_space=pltpu.VMEM)
ANY = pl.BlockSpec(memory_space=pltpu.HBM)


def call(body, outputs, scratch, *operands, flops=0, placed=(), far=0):
    moved = sum(x.size * x.dtype.itemsize for x in (*operands, *outputs))
    return pl.pallas_call(
        body,
        out_shape=outputs,
        in_specs=[VMEM] * (len(operands) - far) + [ANY] * far,
        out_specs=[ANY if i in placed else VMEM for i in range(len(outputs))],
        scratch_shapes=scratch,
        compiler_params=pltpu.CompilerParams(vmem_limit_bytes=40 * 2**20),
        cost_estimate=pl.CostEstimate(flops=flops, bytes_accessed=moved, transcendentals=0),
    )(*operands)


def of(shape, dtype=jnp.bfloat16):
    return jax.ShapeDtypeStruct(shape, dtype)


def ring(value, axis, step):
    peers = lax.axis_size(axis)
    return lax.ppermute(value, axis, [(i, (i + step) % peers) for i in range(peers)])


def across(value, step):
    rows, cols = lax.axis_size("row"), lax.axis_size("col")
    place = lambda pair, row, col: (pair * rows + row) * cols + col
    pairs = [
        (place(pair, row, col), place(1 - pair, row + step, col))
        for pair in range(2)
        for row in range(rows)
        if 0 <= row + step < rows
        for col in range(cols)
    ]
    return lax.ppermute(value, ("pair", "row", "col"), pairs)


def shards(features, offsets, fractions, tissue, w_first, w_second, head_weight):
    _, channels, height, columns = features.shape
    f32, bf16 = jnp.float32, jnp.bfloat16
    row, col = lax.axis_index("row"), lax.axis_index("col")
    rows, cols = lax.axis_size("row"), lax.axis_size("col")
    ring_lane = jnp.arange(RING)[None]
    inside = ((col > 0) | (ring_lane != RING - 1)) & ((col < cols - 1) | (ring_lane != LANES))
    line = jnp.arange(8)[:, None]
    keep = (inside & ((line != 1) | (row > 0)) & ((line != 2) | (row < rows - 1))).astype(f32)

    swap = [(0, 1), (1, 0)]
    tile_shape = (height, channels, columns)
    scratch = [pltpu.VMEM((height * channels, columns), f32)]
    own_tile, edge = call(pack_kernel, [of(tile_shape), of((3, channels, columns))], scratch, features[0])
    from_left = ring(edge, "col", 1)
    from_right = ring(edge, "col", -1)
    other_tile = lax.ppermute(own_tile, "pair", swap)
    lane = jnp.arange(columns)
    group = jnp.arange(len(GROUPS))[:, None, None]
    is_left = jnp.where((group == 1) & (lane >= 2 * PITCH), (lane - 2 * PITCH) % (2 * REACH) < REACH, lane % PITCH < HALO)
    joined = jnp.where(
        is_left,
        jnp.where(col == 0, jnp.zeros_like(from_left), from_left),
        jnp.where(col == cols - 1, jnp.zeros_like(from_right), from_right),
    )
    both_joined = lax.all_gather(joined, "pair")
    other_joined = jnp.where(lax.axis_index("pair") == 0, both_joined[1], both_joined[0])
    mixed = jnp.where(lane < 2 * PITCH, other_joined[1], joined[1])
    folded = jnp.concatenate([mixed[: channels // 2, : columns // 2], mixed[channels // 2 :, : columns // 2]], axis=1)

    def message(*parts):
        return jnp.concatenate([*(part.reshape(-1, columns) for part in parts), folded])

    above = across(message(other_tile[height - HALO :], own_tile[height - REACH :], other_joined[2]), 1)
    below = across(message(other_tile[:HALO], own_tile[:REACH], other_joined[0]), -1)

    wide = height * channels
    band, side, near, base, cover, first_w, second_w, sums, inner_motion, hats, head = call(
        middle_kernel,
        [
            of((wide, RING)),
            of((8 * channels, RING)),
            of((4 * channels, RING)),
            of((2, height, columns), f32),
            of((height, columns), f32),
            of((3 * channels, 6 * channels)),
            of((3 * channels, 3 * channels)),
            of(((height // 2 - 2) * channels, RING), f32),
            of((2, height, columns), f32),
            of((height // 2 - 2, RING, RING)),
            of(head_weight.shape),
        ],
        [
            pltpu.VMEM((2 * wide, RING), bf16),
            pltpu.VMEM(((height - 2) * channels, RING), bf16),
            pltpu.VMEM((channels, (height - 4) * columns), bf16),
            pltpu.VMEM((2, height, columns), f32),
            pltpu.VMEM(tissue.shape[1:], jnp.int32),
            pltpu.SemaphoreType.DMA((2,)),
        ],
        keep, own_tile, other_tile, joined, other_joined,
        w_first, w_second, offsets[0], fractions[0], head_weight, tissue[0],
        flops=4 * 10**9, far=2,
    )
    common = (keep, band, side, near, base, cover, first_w, second_w, sums, inner_motion, hats)
    edge_scratch = [
        pltpu.VMEM((HALO * channels, RING), bf16),
        pltpu.VMEM((8 * channels, RING), bf16),
        pltpu.VMEM((4 * channels, RING), bf16),
        pltpu.VMEM((channels, 2 * columns), bf16),
        pltpu.VMEM((2, height // 2, columns), f32),
    ]
    top, top_motion = call(
        top_kernel,
        [of((5 * channels, RING), f32), of((2, height // 2, columns), f32)],
        edge_scratch,
        *common, above, head,
        flops=10**9,
    )
    warped, motion = call(
        bottom_kernel,
        [of((channels, height, columns)), of((2, height, columns), f32)],
        [
            *edge_scratch,
            pltpu.VMEM((2, height, columns), f32),
            pltpu.VMEM((wide, columns), f32),
            pltpu.VMEM((channels, height, columns), bf16),
            pltpu.SemaphoreType.DMA((6,)),
        ],
        *common, top, top_motion, below, head,
        flops=10**9, placed=(0, 1),
    )
    return (warped[None], motion[None])


def solution(mesh):
    return jax.shard_map(
        shards,
        mesh=mesh,
        in_specs=(
            P("pair", None, "row", "col"),
            P("pair", None, "row", "col"),
            P("pair", None, "row", "col"),
            P("pair", "row", "col"),
            P(),
            P(),
            P(),
        ),
        out_specs=(P("pair", None, "row", "col"), P("pair", None, "row", "col")),
        check_vma=False,
    )
```

```python
import functools

import jax
import jax.numpy as jnp
from jax import lax
from jax.experimental import pallas as pl
from jax.experimental.pallas import tpu as pltpu
from jax.sharding import PartitionSpec as P

MAXS = 8
BLK = 8
CH = 64
HALO = MAXS + 1
LANES = 128
REACH = 2
RING = 2 * LANES
PITCH = 2 * HALO
GROUPS = ((0, 7), (7, 9), (9, 16))


VECTOR = (0, 2, 1)
frac_scale = 256.0


def lane_iota(shape):
    return lax.broadcasted_iota(jnp.int32, shape, len(shape) - 1)


def middle_of(slot):
    return PITCH * slot + HALO


def middle_of_extra(index):
    return 2 * PITCH + 2 * REACH * index + REACH


def border_of(vector, at):
    return pltpu.roll(vector, -at % LANES, 1)


def pack_kernel(feat_ref, tile_ref, edge_ref, rows_ref):
    channels, height, lanes = feat_ref.shape
    for ch in range(channels):
        rows_ref[pl.ds(ch * height, height), :] = feat_ref[ch].astype(jnp.float32)
    lane = lane_iota((channels, lanes))
    for group, (first, last) in enumerate(GROUPS):
        packed = jnp.zeros((channels, lanes), jnp.float32)
        taken = [(row, middle_of(row - first), HALO) for row in range(first, last)]
        if group == 1:
            taken += [(row, middle_of_extra(i), REACH) for i, row in enumerate((0, 1, height - 2, height - 1))]
        for row, at, wide in taken:
            value = rows_ref[pl.ds(row, channels, stride=height), :]
            if wide == HALO:
                tile_ref[row] = value.astype(jnp.bfloat16)
            packed = jnp.where((lane >= at - wide) & (lane < at + wide), pltpu.roll(value, at % lanes, 1), packed)
        if group == 1:
            half = channels // 2
            packed = jnp.where(lane[:half] < lanes // 2, packed[:half], pltpu.roll(packed[half:], lanes // 2, 1))
        edge_ref[pl.ds(VECTOR[group] * channels, packed.shape[0]), :] = packed.astype(jnp.bfloat16)


def shifted_sum(stacked):
    count = stacked.shape[0] // 3
    left = pltpu.roll(stacked[:count], 1, 1)
    right = pltpu.roll(stacked[2 * count :], RING - 1, 1)
    return left + stacked[count : 2 * count] + right


def hidden_row(taken, first_w_ref, keep):
    total = jnp.dot(first_w_ref[...], taken, preferred_element_type=jnp.float32)
    return (jnp.maximum(shifted_sum(total), 0.0) * keep).astype(jnp.bfloat16)


def second_row(taken, second_w_ref):
    total = jnp.dot(second_w_ref[...], taken, preferred_element_type=jnp.float32)
    return jnp.maximum(shifted_sum(total)[:, :LANES], 0.0).astype(jnp.bfloat16)


def project(second_ref, rows, head_ref, residual_ref):
    pairs = jnp.dot(head_ref[...], second_ref[...], preferred_element_type=jnp.float32)
    for index, row in enumerate(rows):
        for k in range(2):
            residual_ref[k, pl.ds(row, 1), :] = pairs[k : k + 1, index * LANES : (index + 1) * LANES]


def two_rows(motion_ref, k, row):
    return jnp.concatenate([motion_ref[k, row : row + 1, :], motion_ref[k, row + 1 : row + 2, :]], axis=1)


def column_weights(motion_ref, row):
    place = (lane_iota((1, RING)) & (LANES - 1)).astype(jnp.float32) + two_rows(motion_ref, 1, row)
    parts = []
    for first, count in ((0, LANES + 16), (-16, 16)):
        column = (lax.broadcasted_iota(jnp.int32, (count, RING), 0) + first).astype(jnp.float32)
        parts.append(jnp.maximum(1.0 - jnp.abs(place - column), 0.0).astype(jnp.bfloat16))
    return jnp.concatenate([parts[0], jnp.zeros((RING - LANES - 32, RING), jnp.bfloat16), parts[1]])


def warp_part(motion_ref, row, hat, source, first, count, total):
    mixed = jnp.dot(source, hat, preferred_element_type=jnp.float32)
    place = jnp.where(lane_iota((1, RING)) < LANES, 0.0, 1.0) + two_rows(motion_ref, 0, row)
    channels = source.shape[0] // count
    for step in range(count):
        weight = jnp.maximum(1.0 - jnp.abs(place - (first + step - row)), 0.0)
        term = weight * mixed[step * channels : (step + 1) * channels]
        total = term if total is None else total + term
    return total


def lay_both(tile, vector, at, *targets):
    border = border_of(vector, at).astype(jnp.bfloat16)
    for ref, start in targets:
        block = pl.ds(start, tile.shape[0])
        ref[block, :LANES] = tile
        ref[block, LANES:] = border


def middle_kernel(
    keep_ref, own_tile_ref, other_tile_ref, own_joined_ref, other_joined_ref,
    w_first_ref, w_second_ref, offsets_ref, fractions_ref, head_in_ref, tissue_in_ref,
    band_ref, side_ref, near_ref, base_ref, cover_ref, first_w_ref, second_w_ref, sums_ref, motion_ref, hats_ref, head_ref,
    window_ref, hidden_ref, second_ref, part_ref, tissue_ref, sems,
):
    height, channels, lanes = own_tile_ref.shape
    copies = [
        pltpu.make_async_copy(head_in_ref, head_ref, sems.at[0]),
        pltpu.make_async_copy(tissue_in_ref, tissue_ref, sems.at[1]),
    ]
    for copy in copies:
        copy.start()
    both = 2 * channels
    for b in range(3):
        block = pl.ds(b * channels, channels)
        for a in range(3):
            first_w_ref[block, a * both : (a + 1) * both] = w_first_ref[3 * a + b]
        second_w_ref[block, :both] = jnp.concatenate([w_second_ref[b], w_second_ref[3 + b]], axis=1)
        second_w_ref[block, both:] = w_second_ref[6 + b]
    for group, (first, last) in enumerate(GROUPS):
        own_vector = group_vector(own_joined_ref, group, channels)
        other_vector = group_vector(other_joined_ref, group, channels)
        for row in range(first, last):
            lay_both(own_tile_ref[row], own_vector, middle_of(row - first), (band_ref, row * channels), (window_ref, row * both))
            lay_both(other_tile_ref[row], other_vector, middle_of(row - first), (window_ref, row * both + channels))
    side_ref[: 2 * both] = window_ref[: 2 * both]
    side_ref[2 * both :] = window_ref[(height - 2) * both :]
    keep = keep_ref[0:1]
    for row in range(1, height - 1):
        taken = window_ref[pl.ds((row - 1) * both, 3 * both), :]
        hidden_ref[pl.ds((row - 1) * channels, channels), :] = hidden_row(taken, first_w_ref, keep)
    near_ref[:both] = hidden_ref[:both]
    near_ref[both:] = hidden_ref[(height - 4) * channels :]
    part_ref[...] = jnp.zeros_like(part_ref)
    inner = range(2, height - 2)
    for index in range(len(inner)):
        taken = hidden_ref[pl.ds(index * channels, 3 * channels), :]
        second_ref[:, index * lanes : (index + 1) * lanes] = second_row(taken, second_w_ref)
    for copy in copies:
        copy.wait()
    project(second_ref, inner, head_ref, part_ref)

    cells = tissue_ref[...].astype(jnp.float32)
    count = cells.shape[1]
    spread = lax.broadcasted_iota(jnp.int32, (count, lanes), 1) // BLK == lax.broadcasted_iota(jnp.int32, (count, lanes), 0)
    spread = jnp.dot(cells, spread.astype(jnp.float32), preferred_element_type=jnp.float32)
    for cell in range(cells.shape[0]):
        cover_ref[pl.ds(cell * BLK, BLK), :] = jnp.broadcast_to(spread[cell : cell + 1], (BLK, lanes))
    base_ref[...] = offsets_ref[...].astype(jnp.float32) + fractions_ref[...].astype(jnp.float32) / frac_scale
    motion_ref[...] = base_ref[...] + cover_ref[...][None] * jnp.tanh(part_ref[...])
    for row in range(2, height - 2, 2):
        first, last = max(0, row - HALO), min(height, row + HALO + 2)
        source = band_ref[pl.ds(first * channels, (last - first) * channels), :]
        hat = column_weights(motion_ref, row)
        hats_ref[row // 2 - 1] = hat
        sums_ref[pl.ds((row // 2 - 1) * channels, channels), :] = warp_part(
            motion_ref, row, hat, source, first, last - first, None
        )


def new_motion(side_ref, hidden_ref, second_ref, rows, keeps, spots, weights, field_refs, half, inner_motion_ref, residual_ref):
    first_w_ref, second_w_ref, head_ref = weights
    base_ref, cover_ref = field_refs
    both = side_ref.shape[0] // 4
    channels = both // 2
    for index, (keep, spot) in enumerate(zip(keeps, spots)):
        taken = side_ref[pl.ds(index * both, 3 * both), :]
        hidden_ref[pl.ds(spot * channels, channels), :] = hidden_row(taken, first_w_ref, keep)
    for index in range(2):
        taken = hidden_ref[pl.ds(index * channels, 3 * channels), :]
        second_ref[:, index * LANES : (index + 1) * LANES] = second_row(taken, second_w_ref)
    residual_ref[...] = jnp.zeros_like(residual_ref)
    project(second_ref, rows, head_ref, residual_ref)
    count = residual_ref.shape[1]
    block = pl.ds(half * count, count)
    fresh = base_ref[:, block, :] + cover_ref[block, :][None] * jnp.tanh(residual_ref[...])
    place = lax.broadcasted_iota(jnp.int32, fresh.shape, 1)
    is_fresh = (place == rows[0]) | (place == rows[1])
    return jnp.where(is_fresh, fresh, inner_motion_ref[:, block, :])


def message_row(ref, index, channels):
    return ref[pl.ds(index * channels, channels), :]


def unfolded(ref, start):
    folded = ref[start:, :].astype(jnp.float32)
    return jnp.concatenate([folded, pltpu.roll(folded, LANES // 2, 1)])


def message_borders(ref, channels):
    return message_row(ref, HALO + 2, channels).astype(jnp.float32), unfolded(ref, (HALO + 3) * channels)


def group_vector(ref, group, channels):
    if group == 1:
        return unfolded(ref, VECTOR[group] * channels)
    return message_row(ref, VECTOR[group], channels).astype(jnp.float32)


def top_kernel(
    keep_ref, band_ref, near_side_ref, near_ref, base_ref, cover_ref, first_w_ref, second_w_ref, sums_ref,
    inner_motion_ref, hats_ref, above_ref, head_ref,
    top_ref, motion_ref, halo_ref, side_ref, hidden_ref, second_ref, residual_ref,
):
    channels = head_ref.shape[1]
    both = 2 * channels
    seven, two = message_borders(above_ref, channels)
    for index in range(HALO):
        targets = [(halo_ref, index * channels)]
        if index >= HALO - 2:
            targets.append((side_ref, (index - HALO + 2) * both))
        strip = (two, middle_of(index)) if index < 2 else (seven, middle_of(index - 2))
        lay_both(message_row(above_ref, index, channels), *strip, *targets)
    for index in range(2):
        tile = message_row(above_ref, HALO + index, channels)
        lay_both(tile, two, middle_of_extra(2 + index), (side_ref, index * both + channels))
    side_ref[2 * both :] = near_side_ref[: 2 * both]
    hidden_ref[both:] = near_ref[:both]
    keeps = (keep_ref[1:2], keep_ref[0:1])
    weights = (first_w_ref, second_w_ref, head_ref)
    motion_ref[...] = new_motion(
        side_ref, hidden_ref, second_ref, (0, 1), keeps, (0, 1), weights, (base_ref, cover_ref), 0, inner_motion_ref, residual_ref
    )
    for row in (2, 4, 6, 8):
        total = sums_ref[pl.ds((row // 2 - 1) * channels, channels), :]
        source = halo_ref[row * channels :, :]
        total = warp_part(inner_motion_ref, row, hats_ref[row // 2 - 1], source, row - HALO, HALO - row, total)
        top_ref[pl.ds(row // 2 * channels, channels), :] = total
    hat = column_weights(motion_ref, 0)
    total = warp_part(motion_ref, 0, hat, halo_ref[...], -HALO, HALO, None)
    top_ref[:channels, :] = warp_part(motion_ref, 0, hat, band_ref[: (HALO + 2) * channels, :], 0, HALO + 2, total)


def bottom_kernel(
    keep_ref, band_ref, near_side_ref, near_ref, base_ref, cover_ref, first_w_ref, second_w_ref, sums_ref,
    inner_motion_ref, hats_ref, top_ref, top_motion_ref, below_ref, head_ref,
    warped_ref, field_ref, halo_ref, side_ref, hidden_ref, second_ref, residual_ref, motion_ref, rows_ref, staged_ref, sems,
):
    channels, height, lanes = warped_ref.shape
    both = 2 * channels
    half = height // 2
    seven, two = message_borders(below_ref, channels)
    for index in range(HALO):
        targets = [(halo_ref, index * channels)]
        if index < 2:
            targets.append((side_ref, (2 + index) * both))
        strip = (seven, middle_of(index)) if index < 7 else (two, middle_of(index - 7))
        lay_both(message_row(below_ref, index, channels), *strip, *targets)
    for index in range(2):
        tile = message_row(below_ref, HALO + index, channels)
        lay_both(tile, two, middle_of_extra(index), (side_ref, (2 + index) * both + channels))
    side_ref[: 2 * both] = near_side_ref[2 * both :]
    hidden_ref[:both] = near_ref[both:]
    keeps = (keep_ref[0:1], keep_ref[2:3])
    weights = (first_w_ref, second_w_ref, head_ref)
    motion_ref[:, :half, :] = top_motion_ref[...]
    motion_ref[:, half:, :] = new_motion(
        side_ref, hidden_ref, second_ref, (half - 2, half - 1), keeps, (2, 3), weights, (base_ref, cover_ref), 1,
        inner_motion_ref, residual_ref,
    )
    field_copy = pltpu.make_async_copy(motion_ref, field_ref, sems.at[4])
    field_copy.start()

    def keep_rows(row, total):
        rows_ref[pl.ds(row * channels, channels), :] = total[:, :lanes]
        rows_ref[pl.ds((row + 1) * channels, channels), :] = total[:, lanes:]

    for row in (0, 2, 4):
        keep_rows(row, top_ref[pl.ds(row // 2 * channels, channels), :])
    for row in (6, 8, 10, 12):
        if row < HALO:
            total = top_ref[pl.ds(row // 2 * channels, channels), :]
        else:
            total = sums_ref[pl.ds((row // 2 - 1) * channels, channels), :]
        count = row + HALO + 2 - height
        source = halo_ref[: count * channels, :]
        keep_rows(row, warp_part(inner_motion_ref, row, hats_ref[row // 2 - 1], source, height, count, total))
        if row == 6:
            for ch in range(channels):
                value = rows_ref[pl.ds(ch, half, stride=channels), :]
                staged_ref[ch, :half, :] = value.astype(jnp.bfloat16)
            upper = pl.ds(0, half)
            upper_copy = pltpu.make_async_copy(staged_ref.at[:, upper], warped_ref.at[:, upper], sems.at[5])
            upper_copy.start()
    row = height - 2
    start = row - HALO
    hat = column_weights(motion_ref, row)
    total = warp_part(motion_ref, row, hat, band_ref[start * channels :, :], start, HALO + 2, None)
    keep_rows(row, warp_part(motion_ref, row, hat, halo_ref[...], height, HALO, total))
    copies = []
    piece = channels // 4
    for part in range(4):
        for ch in range(part * piece, (part + 1) * piece):
            value = rows_ref[pl.ds(half * channels + ch, half, stride=channels), :]
            staged_ref[ch, half:, :] = value.astype(jnp.bfloat16)
        block, lower = pl.ds(part * piece, piece), pl.ds(half, half)
        copies.append(pltpu.make_async_copy(staged_ref.at[block, lower], warped_ref.at[block, lower], sems.at[part]))
        copies[-1].start()
    for copy in (field_copy, upper_copy, *copies):
        copy.wait()


VMEM = pl.BlockSpec(memory_space=pltpu.VMEM)
ANY = pl.BlockSpec(memory_space=pltpu.HBM)


def call(body, outputs, scratch, *operands, flops=0, placed=(), far=0):
    moved = sum(x.size * x.dtype.itemsize for x in (*operands, *outputs))
    return pl.pallas_call(
        body,
        out_shape=outputs,
        in_specs=[VMEM] * (len(operands) - far) + [ANY] * far,
        out_specs=[ANY if i in placed else VMEM for i in range(len(outputs))],
        scratch_shapes=scratch,
        compiler_params=pltpu.CompilerParams(vmem_limit_bytes=40 * 2**20),
        cost_estimate=pl.CostEstimate(flops=flops, bytes_accessed=moved, transcendentals=0),
    )(*operands)


def of(shape, dtype=jnp.bfloat16):
    return jax.ShapeDtypeStruct(shape, dtype)


def ring(value, axis, step):
    peers = lax.axis_size(axis)
    return lax.ppermute(value, axis, [(i, (i + step) % peers) for i in range(peers)])


def across(value, step):
    rows, cols = lax.axis_size("row"), lax.axis_size("col")
    place = lambda pair, row, col: (pair * rows + row) * cols + col
    pairs = [
        (place(pair, row, col), place(1 - pair, row + step, col))
        for pair in range(2)
        for row in range(rows)
        if 0 <= row + step < rows
        for col in range(cols)
    ]
    return lax.ppermute(value, ("pair", "row", "col"), pairs)


def shards(features, offsets, fractions, tissue, w_first, w_second, head_weight):
    _, channels, height, columns = features.shape
    f32, bf16 = jnp.float32, jnp.bfloat16
    row, col = lax.axis_index("row"), lax.axis_index("col")
    rows, cols = lax.axis_size("row"), lax.axis_size("col")
    ring_lane = jnp.arange(RING)[None]
    inside = ((col > 0) | (ring_lane != RING - 1)) & ((col < cols - 1) | (ring_lane != LANES))
    line = jnp.arange(8)[:, None]
    keep = (inside & ((line != 1) | (row > 0)) & ((line != 2) | (row < rows - 1))).astype(f32)

    swap = [(0, 1), (1, 0)]
    tile_shape = (height, channels, columns)
    scratch = [pltpu.VMEM((height * channels, columns), f32)]
    own_tile, edge = call(pack_kernel, [of(tile_shape), of((5 * channels // 2, columns))], scratch, features[0])
    from_left = ring(edge, "col", 1)
    from_right = ring(edge, "col", -1)
    other_tile = lax.ppermute(own_tile, "pair", swap)
    lane, line = jnp.arange(columns), jnp.arange(edge.shape[0])[:, None]
    place = jnp.where(line < 2 * channels, lane, lane % (columns // 2))
    is_extra = (line >= 2 * channels) & (place >= 2 * PITCH)
    is_left = jnp.where(is_extra, (place - 2 * PITCH) % (2 * REACH) < REACH, place % PITCH < HALO)
    masks = jnp.stack([is_left & (col > 0), ~is_left & (col < cols - 1)]).astype(bf16)
    from_where = lax.optimization_barrier(masks)
    zero = jnp.zeros_like(from_left)
    joined = jnp.where(from_where[0] > 0, from_left, jnp.where(from_where[1] > 0, from_right, zero))
    both_joined = lax.all_gather(joined, "pair")
    other_joined = jnp.where(lax.axis_index("pair") == 0, both_joined[1], both_joined[0])
    start = 2 * channels
    mixed = jnp.where(lane % (columns // 2) < 2 * PITCH, other_joined[start:], joined[start:])

    def message(vector, *parts):
        return jnp.concatenate([*(part.reshape(-1, columns) for part in parts), vector, mixed])

    above = across(message(other_joined[channels:start], other_tile[height - HALO :], own_tile[height - REACH :]), 1)
    below = across(message(other_joined[:channels], other_tile[:HALO], own_tile[:REACH]), -1)

    wide = height * channels
    band, side, near, base, cover, first_w, second_w, sums, inner_motion, hats, head = call(
        middle_kernel,
        [
            of((wide, RING)),
            of((8 * channels, RING)),
            of((4 * channels, RING)),
            of((2, height, columns), f32),
            of((height, columns), f32),
            of((3 * channels, 6 * channels)),
            of((3 * channels, 3 * channels)),
            of(((height // 2 - 2) * channels, RING), f32),
            of((2, height, columns), f32),
            of((height // 2 - 2, RING, RING)),
            of(head_weight.shape),
        ],
        [
            pltpu.VMEM((2 * wide, RING), bf16),
            pltpu.VMEM(((height - 2) * channels, RING), bf16),
            pltpu.VMEM((channels, (height - 4) * columns), bf16),
            pltpu.VMEM((2, height, columns), f32),
            pltpu.VMEM(tissue.shape[1:], jnp.int32),
            pltpu.SemaphoreType.DMA((2,)),
        ],
        keep, own_tile, other_tile, joined, other_joined,
        w_first, w_second, offsets[0], fractions[0], head_weight, tissue[0],
        flops=4 * 10**9, far=2,
    )
    common = (keep, band, side, near, base, cover, first_w, second_w, sums, inner_motion, hats)
    edge_scratch = [
        pltpu.VMEM((HALO * channels, RING), bf16),
        pltpu.VMEM((8 * channels, RING), bf16),
        pltpu.VMEM((4 * channels, RING), bf16),
        pltpu.VMEM((channels, 2 * columns), bf16),
        pltpu.VMEM((2, height // 2, columns), f32),
    ]
    top, top_motion = call(
        top_kernel,
        [of((5 * channels, RING), f32), of((2, height // 2, columns), f32)],
        edge_scratch,
        *common, above, head,
        flops=10**9,
    )
    warped, motion = call(
        bottom_kernel,
        [of((channels, height, columns)), of((2, height, columns), f32)],
        [
            *edge_scratch,
            pltpu.VMEM((2, height, columns), f32),
            pltpu.VMEM((wide, columns), f32),
            pltpu.VMEM((channels, height, columns), bf16),
            pltpu.SemaphoreType.DMA((6,)),
        ],
        *common, top, top_motion, below, head,
        flops=10**9, placed=(0, 1),
    )
    return (warped[None], motion[None])


def solution(mesh):
    return jax.shard_map(
        shards,
        mesh=mesh,
        in_specs=(
            P("pair", None, "row", "col"),
            P("pair", None, "row", "col"),
            P("pair", None, "row", "col"),
            P("pair", "row", "col"),
            P(),
            P(),
            P(),
        ),
        out_specs=(P("pair", None, "row", "col"), P("pair", None, "row", "col")),
        check_vma=False,
    )
```

```python
import functools

import jax
import jax.numpy as jnp
from jax import lax
from jax.experimental import pallas as pl
from jax.experimental.pallas import tpu as pltpu
from jax.sharding import PartitionSpec as P

MAXS = 8
BLK = 8
CH = 64
HALO = MAXS + 1
LANES = 128
REACH = 2
RING = 2 * LANES
PITCH = 2 * HALO
GROUPS = ((0, 7), (7, 9), (9, 16))


VECTOR = (0, 2, 1)
frac_scale = 256.0


def lane_iota(shape):
    return lax.broadcasted_iota(jnp.int32, shape, len(shape) - 1)


def middle_of(slot):
    return PITCH * slot + HALO


def middle_of_extra(index):
    return 2 * PITCH + 2 * REACH * index + REACH


def border_of(vector, at):
    return pltpu.roll(vector, -at % LANES, 1)


def pack_kernel(feat_ref, tile_ref, edge_ref, rows_ref):
    channels, height, lanes = feat_ref.shape
    for ch in range(channels):
        rows_ref[pl.ds(ch * height, height), :] = feat_ref[ch].astype(jnp.float32)
    lane = lane_iota((channels, lanes))
    for group, (first, last) in enumerate(GROUPS):
        packed = jnp.zeros((channels, lanes), jnp.float32)
        taken = [(row, middle_of(row - first), HALO) for row in range(first, last)]
        if group == 1:
            taken += [(row, middle_of_extra(i), REACH) for i, row in enumerate((0, 1, height - 2, height - 1))]
        for row, at, wide in taken:
            value = rows_ref[pl.ds(row, channels, stride=height), :]
            if wide == HALO:
                tile_ref[row] = value.astype(jnp.bfloat16)
            packed = jnp.where((lane >= at - wide) & (lane < at + wide), pltpu.roll(value, at % lanes, 1), packed)
        if group == 1:
            half = channels // 2
            packed = jnp.where(lane[:half] < lanes // 2, packed[:half], pltpu.roll(packed[half:], lanes // 2, 1))
        edge_ref[pl.ds(VECTOR[group] * channels, packed.shape[0]), :] = packed.astype(jnp.bfloat16)


def shifted_sum(stacked):
    count = stacked.shape[0] // 3
    left = pltpu.roll(stacked[:count], 1, 1)
    right = pltpu.roll(stacked[2 * count :], RING - 1, 1)
    return left + stacked[count : 2 * count] + right


def keep_of(sides_ref, line=None):
    def flag(index):
        return jnp.concatenate([sides_ref[index : index + 1, :]] * 2, axis=1)

    lane = lane_iota((1, RING))
    keep = jnp.where(lane == RING - 1, flag(5), jnp.where(lane == LANES, flag(6), 1.0))
    return keep if line is None else keep * flag(line)


def hidden_row(taken, first_w_ref, keep):
    total = jnp.dot(first_w_ref[...], taken, preferred_element_type=jnp.float32)
    return (jnp.maximum(shifted_sum(total), 0.0) * keep).astype(jnp.bfloat16)


def second_row(taken, second_w_ref):
    total = jnp.dot(second_w_ref[...], taken, preferred_element_type=jnp.float32)
    return jnp.maximum(shifted_sum(total)[:, :LANES], 0.0).astype(jnp.bfloat16)


def project(second_ref, rows, head_ref, residual_ref):
    pairs = jnp.dot(head_ref[...], second_ref[...], preferred_element_type=jnp.float32)
    for index, row in enumerate(rows):
        for k in range(2):
            residual_ref[k, pl.ds(row, 1), :] = pairs[k : k + 1, index * LANES : (index + 1) * LANES]


def two_rows(motion_ref, k, row):
    return jnp.concatenate([motion_ref[k, row : row + 1, :], motion_ref[k, row + 1 : row + 2, :]], axis=1)


def column_weights(motion_ref, row):
    place = (lane_iota((1, RING)) & (LANES - 1)).astype(jnp.float32) + two_rows(motion_ref, 1, row)
    parts = []
    for first, count in ((0, LANES + 16), (-16, 16)):
        column = (lax.broadcasted_iota(jnp.int32, (count, RING), 0) + first).astype(jnp.float32)
        parts.append(jnp.maximum(1.0 - jnp.abs(place - column), 0.0).astype(jnp.bfloat16))
    return jnp.concatenate([parts[0], jnp.zeros((RING - LANES - 32, RING), jnp.bfloat16), parts[1]])


def warp_part(motion_ref, row, hat, source, first, count, total):
    mixed = jnp.dot(source, hat, preferred_element_type=jnp.float32)
    place = jnp.where(lane_iota((1, RING)) < LANES, 0.0, 1.0) + two_rows(motion_ref, 0, row)
    channels = source.shape[0] // count
    for step in range(count):
        weight = jnp.maximum(1.0 - jnp.abs(place - (first + step - row)), 0.0)
        term = weight * mixed[step * channels : (step + 1) * channels]
        total = term if total is None else total + term
    return total


def lay_both(tile, vector, at, *targets):
    border = border_of(vector, at).astype(jnp.bfloat16)
    for ref, start in targets:
        block = pl.ds(start, tile.shape[0])
        ref[block, :LANES] = tile
        ref[block, LANES:] = border


def middle_kernel(
    sides_ref, own_tile_ref, other_tile_ref, own_joined_ref, other_joined_ref,
    w_first_ref, w_second_ref, offsets_ref, fractions_ref, head_in_ref, tissue_in_ref,
    band_ref, side_ref, near_ref, base_ref, cover_ref, first_w_ref, second_w_ref, sums_ref, motion_ref, hats_ref, head_ref,
    window_ref, hidden_ref, second_ref, part_ref, tissue_ref, sems,
):
    height, channels, lanes = own_tile_ref.shape
    copies = [
        pltpu.make_async_copy(head_in_ref, head_ref, sems.at[0]),
        pltpu.make_async_copy(tissue_in_ref, tissue_ref, sems.at[1]),
    ]
    for copy in copies:
        copy.start()
    both = 2 * channels
    for b in range(3):
        block = pl.ds(b * channels, channels)
        for a in range(3):
            first_w_ref[block, a * both : (a + 1) * both] = w_first_ref[3 * a + b]
        second_w_ref[block, :both] = jnp.concatenate([w_second_ref[b], w_second_ref[3 + b]], axis=1)
        second_w_ref[block, both:] = w_second_ref[6 + b]
    for group, (first, last) in enumerate(GROUPS):
        own_vector = group_vector(own_joined_ref, group, channels)
        other_vector = group_vector(other_joined_ref, group, channels)
        for row in range(first, last):
            lay_both(own_tile_ref[row], own_vector, middle_of(row - first), (band_ref, row * channels), (window_ref, row * both))
            lay_both(other_tile_ref[row], other_vector, middle_of(row - first), (window_ref, row * both + channels))
    side_ref[: 2 * both] = window_ref[: 2 * both]
    side_ref[2 * both :] = window_ref[(height - 2) * both :]
    keep = keep_of(sides_ref)
    for row in range(1, height - 1):
        taken = window_ref[pl.ds((row - 1) * both, 3 * both), :]
        hidden_ref[pl.ds((row - 1) * channels, channels), :] = hidden_row(taken, first_w_ref, keep)
    near_ref[:both] = hidden_ref[:both]
    near_ref[both:] = hidden_ref[(height - 4) * channels :]
    part_ref[...] = jnp.zeros_like(part_ref)
    inner = range(2, height - 2)
    for index in range(len(inner)):
        taken = hidden_ref[pl.ds(index * channels, 3 * channels), :]
        second_ref[:, index * lanes : (index + 1) * lanes] = second_row(taken, second_w_ref)
    for copy in copies:
        copy.wait()
    project(second_ref, inner, head_ref, part_ref)

    cells = tissue_ref[...].astype(jnp.float32)
    count = cells.shape[1]
    spread = lax.broadcasted_iota(jnp.int32, (count, lanes), 1) // BLK == lax.broadcasted_iota(jnp.int32, (count, lanes), 0)
    spread = jnp.dot(cells, spread.astype(jnp.float32), preferred_element_type=jnp.float32)
    for cell in range(cells.shape[0]):
        cover_ref[pl.ds(cell * BLK, BLK), :] = jnp.broadcast_to(spread[cell : cell + 1], (BLK, lanes))
    base_ref[...] = offsets_ref[...].astype(jnp.float32) + fractions_ref[...].astype(jnp.float32) / frac_scale
    motion_ref[...] = base_ref[...] + cover_ref[...][None] * jnp.tanh(part_ref[...])
    for row in range(2, height - 2, 2):
        first, last = max(0, row - HALO), min(height, row + HALO + 2)
        source = band_ref[pl.ds(first * channels, (last - first) * channels), :]
        hat = column_weights(motion_ref, row)
        hats_ref[row // 2 - 1] = hat
        sums_ref[pl.ds((row // 2 - 1) * channels, channels), :] = warp_part(
            motion_ref, row, hat, source, first, last - first, None
        )


def new_motion(side_ref, hidden_ref, second_ref, rows, keeps, spots, weights, field_refs, half, inner_motion_ref, residual_ref):
    first_w_ref, second_w_ref, head_ref = weights
    base_ref, cover_ref = field_refs
    both = side_ref.shape[0] // 4
    channels = both // 2
    for index, (keep, spot) in enumerate(zip(keeps, spots)):
        taken = side_ref[pl.ds(index * both, 3 * both), :]
        hidden_ref[pl.ds(spot * channels, channels), :] = hidden_row(taken, first_w_ref, keep)
    for index in range(2):
        taken = hidden_ref[pl.ds(index * channels, 3 * channels), :]
        second_ref[:, index * LANES : (index + 1) * LANES] = second_row(taken, second_w_ref)
    residual_ref[...] = jnp.zeros_like(residual_ref)
    project(second_ref, rows, head_ref, residual_ref)
    count = residual_ref.shape[1]
    block = pl.ds(half * count, count)
    fresh = base_ref[:, block, :] + cover_ref[block, :][None] * jnp.tanh(residual_ref[...])
    place = lax.broadcasted_iota(jnp.int32, fresh.shape, 1)
    is_fresh = (place == rows[0]) | (place == rows[1])
    return jnp.where(is_fresh, fresh, inner_motion_ref[:, block, :])


def message_row(ref, index, channels):
    return ref[pl.ds(index * channels, channels), :]


def unfolded(ref, start):
    folded = ref[start:, :].astype(jnp.float32)
    return jnp.concatenate([folded, pltpu.roll(folded, LANES // 2, 1)])


def message_borders(ref, channels):
    return message_row(ref, HALO + 2, channels).astype(jnp.float32), unfolded(ref, (HALO + 3) * channels)


def group_vector(ref, group, channels):
    if group == 1:
        return unfolded(ref, VECTOR[group] * channels)
    return message_row(ref, VECTOR[group], channels).astype(jnp.float32)


def top_kernel(
    sides_ref, band_ref, near_side_ref, near_ref, base_ref, cover_ref, first_w_ref, second_w_ref, sums_ref,
    inner_motion_ref, hats_ref, above_ref, head_ref,
    top_ref, motion_ref, halo_ref, side_ref, hidden_ref, second_ref, residual_ref,
):
    channels = head_ref.shape[1]
    both = 2 * channels
    seven, two = message_borders(above_ref, channels)
    for index in range(HALO):
        targets = [(halo_ref, index * channels)]
        if index >= HALO - 2:
            targets.append((side_ref, (index - HALO + 2) * both))
        strip = (two, middle_of(index)) if index < 2 else (seven, middle_of(index - 2))
        lay_both(message_row(above_ref, index, channels), *strip, *targets)
    for index in range(2):
        tile = message_row(above_ref, HALO + index, channels)
        lay_both(tile, two, middle_of_extra(2 + index), (side_ref, index * both + channels))
    side_ref[2 * both :] = near_side_ref[: 2 * both]
    hidden_ref[both:] = near_ref[:both]
    keeps = (keep_of(sides_ref, 7), keep_of(sides_ref))
    weights = (first_w_ref, second_w_ref, head_ref)
    motion_ref[...] = new_motion(
        side_ref, hidden_ref, second_ref, (0, 1), keeps, (0, 1), weights, (base_ref, cover_ref), 0, inner_motion_ref, residual_ref
    )
    for row in (2, 4, 6, 8):
        total = sums_ref[pl.ds((row // 2 - 1) * channels, channels), :]
        source = halo_ref[row * channels :, :]
        total = warp_part(inner_motion_ref, row, hats_ref[row // 2 - 1], source, row - HALO, HALO - row, total)
        top_ref[pl.ds(row // 2 * channels, channels), :] = total
    hat = column_weights(motion_ref, 0)
    total = warp_part(motion_ref, 0, hat, halo_ref[...], -HALO, HALO, None)
    top_ref[:channels, :] = warp_part(motion_ref, 0, hat, band_ref[: (HALO + 2) * channels, :], 0, HALO + 2, total)


def bottom_kernel(
    sides_ref, band_ref, near_side_ref, near_ref, base_ref, cover_ref, first_w_ref, second_w_ref, sums_ref,
    inner_motion_ref, hats_ref, top_ref, top_motion_ref, below_ref, head_ref,
    warped_ref, field_ref, halo_ref, side_ref, hidden_ref, second_ref, residual_ref, motion_ref, rows_ref, staged_ref, sems,
):
    channels, height, lanes = warped_ref.shape
    both = 2 * channels
    half = height // 2
    seven, two = message_borders(below_ref, channels)
    for index in range(HALO):
        targets = [(halo_ref, index * channels)]
        if index < 2:
            targets.append((side_ref, (2 + index) * both))
        strip = (seven, middle_of(index)) if index < 7 else (two, middle_of(index - 7))
        lay_both(message_row(below_ref, index, channels), *strip, *targets)
    for index in range(2):
        tile = message_row(below_ref, HALO + index, channels)
        lay_both(tile, two, middle_of_extra(index), (side_ref, (2 + index) * both + channels))
    side_ref[: 2 * both] = near_side_ref[2 * both :]
    hidden_ref[:both] = near_ref[both:]
    keeps = (keep_of(sides_ref), keep_of(sides_ref, 8))
    weights = (first_w_ref, second_w_ref, head_ref)
    motion_ref[:, :half, :] = top_motion_ref[...]
    motion_ref[:, half:, :] = new_motion(
        side_ref, hidden_ref, second_ref, (half - 2, half - 1), keeps, (2, 3), weights, (base_ref, cover_ref), 1,
        inner_motion_ref, residual_ref,
    )
    field_copy = pltpu.make_async_copy(motion_ref, field_ref, sems.at[4])
    field_copy.start()

    def keep_rows(row, total):
        rows_ref[pl.ds(row * channels, channels), :] = total[:, :lanes]
        rows_ref[pl.ds((row + 1) * channels, channels), :] = total[:, lanes:]

    for row in (0, 2, 4):
        keep_rows(row, top_ref[pl.ds(row // 2 * channels, channels), :])
    for row in (6, 8, 10, 12):
        if row < HALO:
            total = top_ref[pl.ds(row // 2 * channels, channels), :]
        else:
            total = sums_ref[pl.ds((row // 2 - 1) * channels, channels), :]
        count = row + HALO + 2 - height
        source = halo_ref[: count * channels, :]
        keep_rows(row, warp_part(inner_motion_ref, row, hats_ref[row // 2 - 1], source, height, count, total))
        if row == 6:
            for ch in range(channels):
                value = rows_ref[pl.ds(ch, half, stride=channels), :]
                staged_ref[ch, :half, :] = value.astype(jnp.bfloat16)
            upper = pl.ds(0, half)
            upper_copy = pltpu.make_async_copy(staged_ref.at[:, upper], warped_ref.at[:, upper], sems.at[5])
            upper_copy.start()
    row = height - 2
    start = row - HALO
    hat = column_weights(motion_ref, row)
    total = warp_part(motion_ref, row, hat, band_ref[start * channels :, :], start, HALO + 2, None)
    keep_rows(row, warp_part(motion_ref, row, hat, halo_ref[...], height, HALO, total))
    copies = []
    piece = channels // 4
    for part in range(4):
        for ch in range(part * piece, (part + 1) * piece):
            value = rows_ref[pl.ds(half * channels + ch, half, stride=channels), :]
            staged_ref[ch, half:, :] = value.astype(jnp.bfloat16)
        block, lower = pl.ds(part * piece, piece), pl.ds(half, half)
        copies.append(pltpu.make_async_copy(staged_ref.at[block, lower], warped_ref.at[block, lower], sems.at[part]))
        copies[-1].start()
    for copy in (field_copy, upper_copy, *copies):
        copy.wait()


VMEM = pl.BlockSpec(memory_space=pltpu.VMEM)
ANY = pl.BlockSpec(memory_space=pltpu.HBM)


def call(body, outputs, scratch, *operands, flops=0, placed=(), far=0):
    moved = sum(x.size * x.dtype.itemsize for x in (*operands, *outputs))
    return pl.pallas_call(
        body,
        out_shape=outputs,
        in_specs=[VMEM] * (len(operands) - far) + [ANY] * far,
        out_specs=[ANY if i in placed else VMEM for i in range(len(outputs))],
        scratch_shapes=scratch,
        compiler_params=pltpu.CompilerParams(vmem_limit_bytes=40 * 2**20),
        cost_estimate=pl.CostEstimate(flops=flops, bytes_accessed=moved, transcendentals=0),
    )(*operands)


def of(shape, dtype=jnp.bfloat16):
    return jax.ShapeDtypeStruct(shape, dtype)


def ring(value, axis, step):
    peers = lax.axis_size(axis)
    return lax.ppermute(value, axis, [(i, (i + step) % peers) for i in range(peers)])


def across(value, step):
    rows, cols = lax.axis_size("row"), lax.axis_size("col")
    place = lambda pair, row, col: (pair * rows + row) * cols + col
    pairs = [
        (place(pair, row, col), place(1 - pair, row + step, col))
        for pair in range(2)
        for row in range(rows)
        if 0 <= row + step < rows
        for col in range(cols)
    ]
    return lax.ppermute(value, ("pair", "row", "col"), pairs)


def shards(features, offsets, fractions, tissue, w_first, w_second, head_weight):
    _, channels, height, columns = features.shape
    f32, bf16 = jnp.float32, jnp.bfloat16
    row, col = lax.axis_index("row"), lax.axis_index("col")
    rows, cols = lax.axis_size("row"), lax.axis_size("col")
    swap = [(0, 1), (1, 0)]
    tile_shape = (height, channels, columns)
    scratch = [pltpu.VMEM((height * channels, columns), f32)]
    own_tile, edge = call(pack_kernel, [of(tile_shape), of((5 * channels // 2, columns))], scratch, features[0])
    from_left = ring(edge, "col", 1)
    from_right = ring(edge, "col", -1)
    other_tile = lax.ppermute(own_tile, "pair", swap)
    lane = jnp.arange(columns)
    place = lane % (columns // 2)
    left = lane % PITCH < HALO
    left_folded = jnp.where(place < 2 * PITCH, place % PITCH < HALO, (place - 2 * PITCH) % (2 * REACH) < REACH)
    has_left, has_right = col > 0, col < cols - 1
    sides = [left & has_left, ~left & has_right, left_folded & has_left, ~left_folded & has_right, place < 2 * PITCH]
    sides += [jnp.broadcast_to(flag, lane.shape) for flag in (has_left, has_right, row > 0, row < rows - 1)]
    sides = lax.optimization_barrier(jnp.stack(sides).astype(f32))
    is_folded = jnp.arange(edge.shape[0])[:, None] >= 2 * channels
    from_where = [jnp.where(is_folded, sides[2 + i], sides[i]) > 0 for i in range(2)]
    joined = jnp.where(from_where[0], from_left, jnp.where(from_where[1], from_right, jnp.zeros_like(from_left)))
    both_joined = lax.all_gather(joined, "pair")
    other_joined = jnp.where(lax.axis_index("pair") == 0, both_joined[1], both_joined[0])
    start = 2 * channels
    mixed = jnp.where(sides[4] > 0, other_joined[start:], joined[start:])

    def message(vector, *parts):
        return jnp.concatenate([*(part.reshape(-1, columns) for part in parts), vector, mixed])

    above = across(message(other_joined[channels:start], other_tile[height - HALO :], own_tile[height - REACH :]), 1)
    below = across(message(other_joined[:channels], other_tile[:HALO], own_tile[:REACH]), -1)

    wide = height * channels
    band, side, near, base, cover, first_w, second_w, sums, inner_motion, hats, head = call(
        middle_kernel,
        [
            of((wide, RING)),
            of((8 * channels, RING)),
            of((4 * channels, RING)),
            of((2, height, columns), f32),
            of((height, columns), f32),
            of((3 * channels, 6 * channels)),
            of((3 * channels, 3 * channels)),
            of(((height // 2 - 2) * channels, RING), f32),
            of((2, height, columns), f32),
            of((height // 2 - 2, RING, RING)),
            of(head_weight.shape),
        ],
        [
            pltpu.VMEM((2 * wide, RING), bf16),
            pltpu.VMEM(((height - 2) * channels, RING), bf16),
            pltpu.VMEM((channels, (height - 4) * columns), bf16),
            pltpu.VMEM((2, height, columns), f32),
            pltpu.VMEM(tissue.shape[1:], jnp.int32),
            pltpu.SemaphoreType.DMA((2,)),
        ],
        sides, own_tile, other_tile, joined, other_joined,
        w_first, w_second, offsets[0], fractions[0], head_weight, tissue[0],
        flops=4 * 10**9, far=2,
    )
    common = (sides, band, side, near, base, cover, first_w, second_w, sums, inner_motion, hats)
    edge_scratch = [
        pltpu.VMEM((HALO * channels, RING), bf16),
        pltpu.VMEM((8 * channels, RING), bf16),
        pltpu.VMEM((4 * channels, RING), bf16),
        pltpu.VMEM((channels, 2 * columns), bf16),
        pltpu.VMEM((2, height // 2, columns), f32),
    ]
    top, top_motion = call(
        top_kernel,
        [of((5 * channels, RING), f32), of((2, height // 2, columns), f32)],
        edge_scratch,
        *common, above, head,
        flops=10**9,
    )
    warped, motion = call(
        bottom_kernel,
        [of((channels, height, columns)), of((2, height, columns), f32)],
        [
            *edge_scratch,
            pltpu.VMEM((2, height, columns), f32),
            pltpu.VMEM((wide, columns), f32),
            pltpu.VMEM((channels, height, columns), bf16),
            pltpu.SemaphoreType.DMA((6,)),
        ],
        *common, top, top_motion, below, head,
        flops=10**9, placed=(0, 1),
    )
    return (warped[None], motion[None])


def solution(mesh):
    return jax.shard_map(
        shards,
        mesh=mesh,
        in_specs=(
            P("pair", None, "row", "col"),
            P("pair", None, "row", "col"),
            P("pair", None, "row", "col"),
            P("pair", "row", "col"),
            P(),
            P(),
            P(),
        ),
        out_specs=(P("pair", None, "row", "col"), P("pair", None, "row", "col")),
        check_vma=False,
    )
```

```python
import functools

import jax
import jax.numpy as jnp
from jax import lax
from jax.experimental import pallas as pl
from jax.experimental.pallas import tpu as pltpu
from jax.sharding import PartitionSpec as P

MAXS = 8
BLK = 8
CH = 64
HALO = MAXS + 1
LANES = 128
REACH = 2
RING = 2 * LANES
PITCH = 2 * HALO
GROUPS = ((0, 7), (7, 9), (9, 16))


VECTOR = (0, 2, 1)
frac_scale = 256.0


def lane_iota(shape):
    return lax.broadcasted_iota(jnp.int32, shape, len(shape) - 1)


def middle_of(slot):
    return PITCH * slot + HALO


def middle_of_extra(index):
    return 2 * PITCH + 2 * REACH * index + REACH


def border_of(vector, at):
    return pltpu.roll(vector, -at % LANES, 1)


def pack_kernel(feat_ref, tile_ref, edge_ref, rows_ref):
    channels, height, lanes = feat_ref.shape
    for ch in range(channels):
        rows_ref[pl.ds(ch * height, height), :] = feat_ref[ch].astype(jnp.float32)
    lane = lane_iota((channels, lanes))
    for group, (first, last) in enumerate(GROUPS):
        packed = jnp.zeros((channels, lanes), jnp.float32)
        taken = [(row, middle_of(row - first), HALO) for row in range(first, last)]
        if group == 1:
            taken += [(row, middle_of_extra(i), REACH) for i, row in enumerate((0, 1, height - 2, height - 1))]
        for row, at, wide in taken:
            value = rows_ref[pl.ds(row, channels, stride=height), :]
            if wide == HALO:
                tile_ref[row] = value.astype(jnp.bfloat16)
            packed = jnp.where((lane >= at - wide) & (lane < at + wide), pltpu.roll(value, at % lanes, 1), packed)
        if group == 1:
            half = channels // 2
            packed = jnp.where(lane[:half] < lanes // 2, packed[:half], pltpu.roll(packed[half:], lanes // 2, 1))
        edge_ref[pl.ds(VECTOR[group] * channels, packed.shape[0]), :] = packed.astype(jnp.bfloat16)


def shifted_sum(stacked):
    count = stacked.shape[0] // 3
    left = pltpu.roll(stacked[:count], 1, 1)
    right = pltpu.roll(stacked[2 * count :], RING - 1, 1)
    return left + stacked[count : 2 * count] + right


def hidden_row(taken, first_w_ref, keep):
    total = jnp.dot(first_w_ref[...], taken, preferred_element_type=jnp.float32)
    return (jnp.maximum(shifted_sum(total), 0.0) * keep).astype(jnp.bfloat16)


def second_row(taken, second_w_ref):
    total = jnp.dot(second_w_ref[...], taken, preferred_element_type=jnp.float32)
    return jnp.maximum(shifted_sum(total)[:, :LANES], 0.0).astype(jnp.bfloat16)


def project(second_ref, rows, head_ref, residual_ref):
    pairs = jnp.dot(head_ref[...], second_ref[...], preferred_element_type=jnp.float32)
    for index, row in enumerate(rows):
        for k in range(2):
            residual_ref[k, pl.ds(row, 1), :] = pairs[k : k + 1, index * LANES : (index + 1) * LANES]


def two_rows(motion_ref, k, row):
    return jnp.concatenate([motion_ref[k, row : row + 1, :], motion_ref[k, row + 1 : row + 2, :]], axis=1)


def column_weights(motion_ref, row):
    place = (lane_iota((1, RING)) & (LANES - 1)).astype(jnp.float32) + two_rows(motion_ref, 1, row)
    parts = []
    for first, count in ((0, LANES + 16), (-16, 16)):
        column = (lax.broadcasted_iota(jnp.int32, (count, RING), 0) + first).astype(jnp.float32)
        parts.append(jnp.maximum(1.0 - jnp.abs(place - column), 0.0).astype(jnp.bfloat16))
    return jnp.concatenate([parts[0], jnp.zeros((RING - LANES - 32, RING), jnp.bfloat16), parts[1]])


def warp_part(motion_ref, row, hat, source, first, count, total):
    mixed = jnp.dot(source, hat, preferred_element_type=jnp.float32)
    place = jnp.where(lane_iota((1, RING)) < LANES, 0.0, 1.0) + two_rows(motion_ref, 0, row)
    channels = source.shape[0] // count
    for step in range(count):
        weight = jnp.maximum(1.0 - jnp.abs(place - (first + step - row)), 0.0)
        term = weight * mixed[step * channels : (step + 1) * channels]
        total = term if total is None else total + term
    return total


def lay_both(tile, vector, at, *targets):
    border = border_of(vector, at).astype(jnp.bfloat16)
    for ref, start in targets:
        block = pl.ds(start, tile.shape[0])
        ref[block, :LANES] = tile
        ref[block, LANES:] = border


def middle_kernel(
    keep_ref, own_tile_ref, other_tile_ref, own_joined_ref, other_joined_ref,
    w_first_ref, w_second_ref, offsets_ref, fractions_ref, head_in_ref, tissue_in_ref,
    band_ref, side_ref, near_ref, base_ref, cover_ref, first_w_ref, second_w_ref, sums_ref, motion_ref, hats_ref, head_ref,
    window_ref, hidden_ref, second_ref, part_ref, tissue_ref, sems,
):
    height, channels, lanes = own_tile_ref.shape
    copies = [
        pltpu.make_async_copy(head_in_ref, head_ref, sems.at[0]),
        pltpu.make_async_copy(tissue_in_ref, tissue_ref, sems.at[1]),
    ]
    for copy in copies:
        copy.start()
    both = 2 * channels
    for b in range(3):
        block = pl.ds(b * channels, channels)
        for a in range(3):
            first_w_ref[block, a * both : (a + 1) * both] = w_first_ref[3 * a + b]
        second_w_ref[block, :both] = jnp.concatenate([w_second_ref[b], w_second_ref[3 + b]], axis=1)
        second_w_ref[block, both:] = w_second_ref[6 + b]
    for group, (first, last) in enumerate(GROUPS):
        own_vector = group_vector(own_joined_ref, group, channels)
        other_vector = group_vector(other_joined_ref, group, channels)
        for row in range(first, last):
            lay_both(own_tile_ref[row], own_vector, middle_of(row - first), (band_ref, row * channels), (window_ref, row * both))
            lay_both(other_tile_ref[row], other_vector, middle_of(row - first), (window_ref, row * both + channels))
    side_ref[: 2 * both] = window_ref[: 2 * both]
    side_ref[2 * both :] = window_ref[(height - 2) * both :]
    keep = keep_ref[0:1]
    for row in range(1, height - 1):
        taken = window_ref[pl.ds((row - 1) * both, 3 * both), :]
        hidden_ref[pl.ds((row - 1) * channels, channels), :] = hidden_row(taken, first_w_ref, keep)
    near_ref[:both] = hidden_ref[:both]
    near_ref[both:] = hidden_ref[(height - 4) * channels :]
    part_ref[...] = jnp.zeros_like(part_ref)
    inner = range(2, height - 2)
    for index in range(len(inner)):
        taken = hidden_ref[pl.ds(index * channels, 3 * channels), :]
        second_ref[:, index * lanes : (index + 1) * lanes] = second_row(taken, second_w_ref)
    for copy in copies:
        copy.wait()
    project(second_ref, inner, head_ref, part_ref)

    cells = tissue_ref[...].astype(jnp.float32)
    count = cells.shape[1]
    spread = lax.broadcasted_iota(jnp.int32, (count, lanes), 1) // BLK == lax.broadcasted_iota(jnp.int32, (count, lanes), 0)
    spread = jnp.dot(cells, spread.astype(jnp.float32), preferred_element_type=jnp.float32)
    for cell in range(cells.shape[0]):
        cover_ref[pl.ds(cell * BLK, BLK), :] = jnp.broadcast_to(spread[cell : cell + 1], (BLK, lanes))
    base_ref[...] = offsets_ref[...].astype(jnp.float32) + fractions_ref[...].astype(jnp.float32) / frac_scale
    motion_ref[...] = base_ref[...] + cover_ref[...][None] * jnp.tanh(part_ref[...])
    for row in range(2, height - 2, 2):
        first, last = max(0, row - HALO), min(height, row + HALO + 2)
        source = band_ref[pl.ds(first * channels, (last - first) * channels), :]
        hat = column_weights(motion_ref, row)
        hats_ref[row // 2 - 1] = hat
        sums_ref[pl.ds((row // 2 - 1) * channels, channels), :] = warp_part(
            motion_ref, row, hat, source, first, last - first, None
        )


def new_motion(side_ref, hidden_ref, second_ref, rows, keeps, spots, weights, field_refs, half, inner_motion_ref, residual_ref):
    first_w_ref, second_w_ref, head_ref = weights
    base_ref, cover_ref = field_refs
    both = side_ref.shape[0] // 4
    channels = both // 2
    for index, (keep, spot) in enumerate(zip(keeps, spots)):
        taken = side_ref[pl.ds(index * both, 3 * both), :]
        hidden_ref[pl.ds(spot * channels, channels), :] = hidden_row(taken, first_w_ref, keep)
    for index in range(2):
        taken = hidden_ref[pl.ds(index * channels, 3 * channels), :]
        second_ref[:, index * LANES : (index + 1) * LANES] = second_row(taken, second_w_ref)
    residual_ref[...] = jnp.zeros_like(residual_ref)
    project(second_ref, rows, head_ref, residual_ref)
    count = residual_ref.shape[1]
    block = pl.ds(half * count, count)
    fresh = base_ref[:, block, :] + cover_ref[block, :][None] * jnp.tanh(residual_ref[...])
    place = lax.broadcasted_iota(jnp.int32, fresh.shape, 1)
    is_fresh = (place == rows[0]) | (place == rows[1])
    return jnp.where(is_fresh, fresh, inner_motion_ref[:, block, :])


def message_row(ref, index, channels):
    return ref[pl.ds(index * channels, channels), :]


def unfolded(ref, start):
    folded = ref[start:, :].astype(jnp.float32)
    return jnp.concatenate([folded, pltpu.roll(folded, LANES // 2, 1)])


def message_borders(ref, channels):
    return message_row(ref, HALO + 2, channels).astype(jnp.float32), unfolded(ref, (HALO + 3) * channels)


def group_vector(ref, group, channels):
    if group == 1:
        return unfolded(ref, VECTOR[group] * channels)
    return message_row(ref, VECTOR[group], channels).astype(jnp.float32)


def top_kernel(
    keep_ref, band_ref, near_side_ref, near_ref, base_ref, cover_ref, first_w_ref, second_w_ref, sums_ref,
    inner_motion_ref, hats_ref, above_ref, head_ref,
    top_ref, motion_ref, halo_ref, side_ref, hidden_ref, second_ref, residual_ref,
):
    channels = head_ref.shape[1]
    both = 2 * channels
    seven, two = message_borders(above_ref, channels)
    for index in range(HALO):
        targets = [(halo_ref, index * channels)]
        if index >= HALO - 2:
            targets.append((side_ref, (index - HALO + 2) * both))
        strip = (two, middle_of(index)) if index < 2 else (seven, middle_of(index - 2))
        lay_both(message_row(above_ref, index, channels), *strip, *targets)
    for index in range(2):
        tile = message_row(above_ref, HALO + index, channels)
        lay_both(tile, two, middle_of_extra(2 + index), (side_ref, index * both + channels))
    side_ref[2 * both :] = near_side_ref[: 2 * both]
    hidden_ref[both:] = near_ref[:both]
    keeps = (keep_ref[1:2], keep_ref[0:1])
    weights = (first_w_ref, second_w_ref, head_ref)
    motion_ref[...] = new_motion(
        side_ref, hidden_ref, second_ref, (0, 1), keeps, (0, 1), weights, (base_ref, cover_ref), 0, inner_motion_ref, residual_ref
    )
    for row in (2, 4, 6, 8):
        total = sums_ref[pl.ds((row // 2 - 1) * channels, channels), :]
        source = halo_ref[row * channels :, :]
        total = warp_part(inner_motion_ref, row, hats_ref[row // 2 - 1], source, row - HALO, HALO - row, total)
        top_ref[pl.ds(row // 2 * channels, channels), :] = total
    hat = column_weights(motion_ref, 0)
    total = warp_part(motion_ref, 0, hat, halo_ref[...], -HALO, HALO, None)
    top_ref[:channels, :] = warp_part(motion_ref, 0, hat, band_ref[: (HALO + 2) * channels, :], 0, HALO + 2, total)


def bottom_kernel(
    keep_ref, band_ref, near_side_ref, near_ref, base_ref, cover_ref, first_w_ref, second_w_ref, sums_ref,
    inner_motion_ref, hats_ref, top_ref, top_motion_ref, below_ref, head_ref,
    warped_ref, field_ref, halo_ref, side_ref, hidden_ref, second_ref, residual_ref, motion_ref, rows_ref, staged_ref, sems,
):
    channels, height, lanes = warped_ref.shape
    both = 2 * channels
    half = height // 2
    seven, two = message_borders(below_ref, channels)
    for index in range(HALO):
        targets = [(halo_ref, index * channels)]
        if index < 2:
            targets.append((side_ref, (2 + index) * both))
        strip = (seven, middle_of(index)) if index < 7 else (two, middle_of(index - 7))
        lay_both(message_row(below_ref, index, channels), *strip, *targets)
    for index in range(2):
        tile = message_row(below_ref, HALO + index, channels)
        lay_both(tile, two, middle_of_extra(index), (side_ref, (2 + index) * both + channels))
    side_ref[: 2 * both] = near_side_ref[2 * both :]
    hidden_ref[:both] = near_ref[both:]
    keeps = (keep_ref[0:1], keep_ref[2:3])
    weights = (first_w_ref, second_w_ref, head_ref)
    motion_ref[:, :half, :] = top_motion_ref[...]
    motion_ref[:, half:, :] = new_motion(
        side_ref, hidden_ref, second_ref, (half - 2, half - 1), keeps, (2, 3), weights, (base_ref, cover_ref), 1,
        inner_motion_ref, residual_ref,
    )
    field_copy = pltpu.make_async_copy(motion_ref, field_ref, sems.at[4])
    field_copy.start()

    def keep_rows(row, total):
        rows_ref[pl.ds(row * channels, channels), :] = total[:, :lanes]
        rows_ref[pl.ds((row + 1) * channels, channels), :] = total[:, lanes:]

    for row in (0, 2, 4):
        keep_rows(row, top_ref[pl.ds(row // 2 * channels, channels), :])
    for row in (6, 8, 10, 12):
        if row < HALO:
            total = top_ref[pl.ds(row // 2 * channels, channels), :]
        else:
            total = sums_ref[pl.ds((row // 2 - 1) * channels, channels), :]
        count = row + HALO + 2 - height
        source = halo_ref[: count * channels, :]
        keep_rows(row, warp_part(inner_motion_ref, row, hats_ref[row // 2 - 1], source, height, count, total))
        if row == 6:
            for ch in range(channels):
                value = rows_ref[pl.ds(ch, half, stride=channels), :]
                staged_ref[ch, :half, :] = value.astype(jnp.bfloat16)
            upper = pl.ds(0, half)
            upper_copy = pltpu.make_async_copy(staged_ref.at[:, upper], warped_ref.at[:, upper], sems.at[5])
            upper_copy.start()
    row = height - 2
    start = row - HALO
    hat = column_weights(motion_ref, row)
    total = warp_part(motion_ref, row, hat, band_ref[start * channels :, :], start, HALO + 2, None)
    keep_rows(row, warp_part(motion_ref, row, hat, halo_ref[...], height, HALO, total))
    copies = []
    piece = channels // 2
    for part in range(2):
        for ch in range(part * piece, (part + 1) * piece):
            value = rows_ref[pl.ds(half * channels + ch, half, stride=channels), :]
            staged_ref[ch, half:, :] = value.astype(jnp.bfloat16)
        block, lower = pl.ds(part * piece, piece), pl.ds(half, half)
        copies.append(pltpu.make_async_copy(staged_ref.at[block, lower], warped_ref.at[block, lower], sems.at[part]))
        copies[-1].start()
    for copy in (field_copy, upper_copy, *copies):
        copy.wait()


VMEM = pl.BlockSpec(memory_space=pltpu.VMEM)
ANY = pl.BlockSpec(memory_space=pltpu.HBM)


def call(body, outputs, scratch, *operands, flops=0, placed=(), far=0):
    moved = sum(x.size * x.dtype.itemsize for x in (*operands, *outputs))
    return pl.pallas_call(
        body,
        out_shape=outputs,
        in_specs=[VMEM] * (len(operands) - far) + [ANY] * far,
        out_specs=[ANY if i in placed else VMEM for i in range(len(outputs))],
        scratch_shapes=scratch,
        compiler_params=pltpu.CompilerParams(vmem_limit_bytes=40 * 2**20),
        cost_estimate=pl.CostEstimate(flops=flops, bytes_accessed=moved, transcendentals=0),
    )(*operands)


def of(shape, dtype=jnp.bfloat16):
    return jax.ShapeDtypeStruct(shape, dtype)


def ring(value, axis, step):
    peers = lax.axis_size(axis)
    return lax.ppermute(value, axis, [(i, (i + step) % peers) for i in range(peers)])


def across(value, step):
    rows, cols = lax.axis_size("row"), lax.axis_size("col")
    place = lambda pair, row, col: (pair * rows + row) * cols + col
    pairs = [
        (place(pair, row, col), place(1 - pair, row + step, col))
        for pair in range(2)
        for row in range(rows)
        if 0 <= row + step < rows
        for col in range(cols)
    ]
    return lax.ppermute(value, ("pair", "row", "col"), pairs)


def shards(features, offsets, fractions, tissue, w_first, w_second, head_weight):
    _, channels, height, columns = features.shape
    f32, bf16 = jnp.float32, jnp.bfloat16
    row, col = lax.axis_index("row"), lax.axis_index("col")
    rows, cols = lax.axis_size("row"), lax.axis_size("col")
    ring_lane = jnp.arange(RING)[None]
    inside = ((col > 0) | (ring_lane != RING - 1)) & ((col < cols - 1) | (ring_lane != LANES))
    line = jnp.arange(8)[:, None]
    keep = (inside & ((line != 1) | (row > 0)) & ((line != 2) | (row < rows - 1))).astype(f32)

    swap = [(0, 1), (1, 0)]
    tile_shape = (height, channels, columns)
    scratch = [pltpu.VMEM((height * channels, columns), f32)]
    own_tile, edge = call(pack_kernel, [of(tile_shape), of((5 * channels // 2, columns))], scratch, features[0])
    from_left = ring(edge, "col", 1)
    from_right = ring(edge, "col", -1)
    other_tile = lax.ppermute(own_tile, "pair", swap)
    lane, line = jnp.arange(columns), jnp.arange(edge.shape[0])[:, None]
    place = jnp.where(line < 2 * channels, lane, lane % (columns // 2))
    is_extra = (line >= 2 * channels) & (place >= 2 * PITCH)
    is_left = jnp.where(is_extra, (place - 2 * PITCH) % (2 * REACH) < REACH, place % PITCH < HALO)
    masks = jnp.stack([is_left & (col > 0), ~is_left & (col < cols - 1)]).astype(bf16)
    from_where = lax.optimization_barrier(masks)
    zero = jnp.zeros_like(from_left)
    joined = jnp.where(from_where[0] > 0, from_left, jnp.where(from_where[1] > 0, from_right, zero))
    both_joined = lax.all_gather(joined, "pair")
    other_joined = jnp.where(lax.axis_index("pair") == 0, both_joined[1], both_joined[0])
    start = 2 * channels
    mixed = jnp.where(lane % (columns // 2) < 2 * PITCH, other_joined[start:], joined[start:])

    def message(vector, *parts):
        return jnp.concatenate([*(part.reshape(-1, columns) for part in parts), vector, mixed])

    above = across(message(other_joined[channels:start], other_tile[height - HALO :], own_tile[height - REACH :]), 1)
    below = across(message(other_joined[:channels], other_tile[:HALO], own_tile[:REACH]), -1)

    wide = height * channels
    band, side, near, base, cover, first_w, second_w, sums, inner_motion, hats, head = call(
        middle_kernel,
        [
            of((wide, RING)),
            of((8 * channels, RING)),
            of((4 * channels, RING)),
            of((2, height, columns), f32),
            of((height, columns), f32),
            of((3 * channels, 6 * channels)),
            of((3 * channels, 3 * channels)),
            of(((height // 2 - 2) * channels, RING), f32),
            of((2, height, columns), f32),
            of((height // 2 - 2, RING, RING)),
            of(head_weight.shape),
        ],
        [
            pltpu.VMEM((2 * wide, RING), bf16),
            pltpu.VMEM(((height - 2) * channels, RING), bf16),
            pltpu.VMEM((channels, (height - 4) * columns), bf16),
            pltpu.VMEM((2, height, columns), f32),
            pltpu.VMEM(tissue.shape[1:], jnp.int32),
            pltpu.SemaphoreType.DMA((2,)),
        ],
        keep, own_tile, other_tile, joined, other_joined,
        w_first, w_second, offsets[0], fractions[0], head_weight, tissue[0],
        flops=4 * 10**9, far=2,
    )
    common = (keep, band, side, near, base, cover, first_w, second_w, sums, inner_motion, hats)
    edge_scratch = [
        pltpu.VMEM((HALO * channels, RING), bf16),
        pltpu.VMEM((8 * channels, RING), bf16),
        pltpu.VMEM((4 * channels, RING), bf16),
        pltpu.VMEM((channels, 2 * columns), bf16),
        pltpu.VMEM((2, height // 2, columns), f32),
    ]
    top, top_motion = call(
        top_kernel,
        [of((5 * channels, RING), f32), of((2, height // 2, columns), f32)],
        edge_scratch,
        *common, above, head,
        flops=10**9,
    )
    warped, motion = call(
        bottom_kernel,
        [of((channels, height, columns)), of((2, height, columns), f32)],
        [
            *edge_scratch,
            pltpu.VMEM((2, height, columns), f32),
            pltpu.VMEM((wide, columns), f32),
            pltpu.VMEM((channels, height, columns), bf16),
            pltpu.SemaphoreType.DMA((6,)),
        ],
        *common, top, top_motion, below, head,
        flops=10**9, placed=(0, 1),
    )
    return (warped[None], motion[None])


def solution(mesh):
    return jax.shard_map(
        shards,
        mesh=mesh,
        in_specs=(
            P("pair", None, "row", "col"),
            P("pair", None, "row", "col"),
            P("pair", None, "row", "col"),
            P("pair", "row", "col"),
            P(),
            P(),
            P(),
        ),
        out_specs=(P("pair", None, "row", "col"), P("pair", None, "row", "col")),
        check_vma=False,
    )
```
